128 devices in a mesh: px: 16 (over x, z), py: 8 (over y, core).
Axes of the slice: x: 4, y: 4, z: 4, core: 2. Of those that a mesh axis runs over, the one named last changes fastest.
Arguments:
- state: float32 [16, 8, 8192, 256], P('px', 'py'), may hold values from -6 to 6
- prop_base: float32 [256, 256], replicated, may hold values from -0.375 to 0.375
- prop_height: float32 [256, 256], replicated, may hold values from -0.375 to 0.375
- restrict: float32 [256, 128], replicated, may hold values from -0.375 to 0.375
- lift: float32 [128, 256], replicated, may hold values from -0.5 to 0.5
- layer_id: int32 [16, 8, 8192], P('px', 'py'), may hold values from 0 to 2
- heights: int32 [16, 8, 8192], P('px', 'py'), may hold values from 1 to 4
- degree: int32 [16, 8, 8192], P('px', 'py'), may hold values from 1 to 4
- send_rows: int32 [16, 8, 4, 512], P('px', 'py'), may hold values from 0 to 8191
- recv_rows: int32 [16, 8, 4, 512], P('px', 'py'), may hold values from 0 to 8191
- move_src: int32 [16, 8, 128], P('px', 'py'), may hold values from 0 to 8191, as said below
- move_dst: int32 [16, 8, 128], P('px', 'py'), may hold values from 0 to 127, as said below
- move_slot: int32 [16, 8, 128], P('px', 'py'), may hold values from 0 to 8191, as said below
Outputs:
- new_state: float32 [16, 8, 8192, 256], P('px', 'py')
The draws below stay inside these ranges and needn't reach their ends.
Inputs may be any that keep to these rules, and one draw needn't show every extreme that they name: `move_src`: on each partition the 128 slots are distinct. `move_dst`: each partition hands exactly 2 elements to each of 64 other partitions and none to the rest, and receives exactly 2 elements from each of 64 partitions. `move_slot`: the slots at which a partition's arriving elements land are exactly its own move_src slots, each once.
All inputs are finite; a program needn't handle non-finite values.
Results may differ from the reference program's by a relative error of at most 0.0001.
Values sent between devices are 32-bit elements; how exact they have to be, the bound alone decides.
A program may use at most 128 MiB of HBM per device.

```python
import jax
import jax.numpy as jnp
from jax import lax

NB = 256
NT = 128
E_DEV = 8192
K = 512
LAYERS = 3
PMAX = 4
HMAX = 4
C_MOVE = 2
PARTS_X = 16
PARTS_Y = 8
G = 64
MOVE = 128


def migration_lists(key):
    base_key = jax.random.fold_in(key, 7351)
    count = PARTS_X * PARTS_Y
    keys = jax.random.split(base_key, 4)

    def pick_slots(subkey):
        return jax.random.permutation(subkey, E_DEV)[:MOVE]

    def item_order(subkey):
        return jax.random.permutation(subkey, MOVE)
    vacated = jax.vmap(pick_slots)(jax.random.split(keys[0], count)).astype(jnp.int32)
    label_owner = jax.random.permutation(keys[1], count).astype(jnp.int32)
    owner_label = jnp.zeros((count,), jnp.int32).at[label_owner].set(jnp.arange(count, dtype=jnp.int32))
    steps_away = (jax.random.permutation(keys[2], count - 1)[:G] + 1).astype(jnp.int32)
    ordering = jax.vmap(item_order)(jax.random.split(keys[3], count)).astype(jnp.int32)
    group = ordering // C_MOVE
    within = ordering % C_MOVE
    target = label_owner[(owner_label[:, None] + steps_away[group]) % count]
    landing = vacated[target, group * C_MOVE + within]
    shape = (PARTS_X, PARTS_Y, MOVE)
    return (vacated.reshape(shape), target.reshape(shape), landing.reshape(shape))


def draw_move_src(key, part):
    return migration_lists(key)[0]


def draw_move_dst(key, part):
    return migration_lists(key)[1]


def draw_move_slot(key, part):
    return migration_lists(key)[2]


def place_ends(entries, stream_key, least, largest):
    dims = entries.shape
    place = [jax.random.randint(jax.random.fold_in(stream_key, axis), (), 0, dims[axis]) for axis in range(len(dims))]
    entries = entries.at[tuple(place)].set(least)
    longest = dims.index(max(dims))
    place[longest] = (place[longest] + 1) % dims[longest]
    return entries.at[tuple(place)].set(largest)


def level_of(rng, extent, cuts, low, largest):
    factor_of, own = 1.0, jax.random.fold_in(rng, 6)
    for position, blocks in cuts:
        draws = jnp.exp(jax.random.uniform(jax.random.fold_in(own, position), (blocks,), jnp.float32, low / len(cuts), largest / len(cuts)))
        factor_of = factor_of * jnp.repeat(draws, extent[position] // blocks).reshape([-1 if axis == position else 1 for axis in range(len(extent))])
    return factor_of


def normal_values(stream_key, extent, width, bound, pieces=(), held_as=jnp.bfloat16):
    factor_of = level_of(stream_key, extent, pieces, -0.22, 0.18) if pieces else 1.0
    drawn = jax.random.normal(stream_key, extent, jnp.float32) * width * factor_of
    return jnp.minimum(jnp.maximum(drawn, -bound), bound).astype(held_as)


def setup_inputs(seed: int = 0) -> dict:
    seeds = jax.random.split(jax.random.key(seed), 14)
    return {
        "state": normal_values(seeds[0], (PARTS_X, PARTS_Y, E_DEV, NB), 1.0, 6.0, ((0, 16), (1, 8)), jnp.float32),
        "prop_base": normal_values(seeds[1], (NB, NB), NB ** -0.5, 0.375, (), jnp.float32),
        "prop_height": normal_values(seeds[2], (NB, NB), NB ** -0.5, 0.375, (), jnp.float32),
        "restrict": normal_values(seeds[3], (NB, NT), NB ** -0.5, 0.375, (), jnp.float32),
        "lift": normal_values(seeds[4], (NT, NB), NT ** -0.5, 0.5, (), jnp.float32),
        "layer_id": place_ends(jax.random.randint(seeds[5], (PARTS_X, PARTS_Y, E_DEV), 0, LAYERS), jax.random.fold_in(seeds[5], 1), 0, LAYERS - 1).astype(jnp.int32),
        "heights": place_ends(jax.random.randint(seeds[6], (PARTS_X, PARTS_Y, E_DEV), 1, HMAX + 1), jax.random.fold_in(seeds[6], 1), 1, HMAX).astype(jnp.int32),
        "degree": place_ends(jax.random.randint(seeds[7], (PARTS_X, PARTS_Y, E_DEV), 1, PMAX + 1), jax.random.fold_in(seeds[7], 1), 1, PMAX).astype(jnp.int32),
        "send_rows": place_ends(jax.random.randint(seeds[8], (PARTS_X, PARTS_Y, 4, K), 0, E_DEV), jax.random.fold_in(seeds[8], 1), 0, E_DEV - 1).astype(jnp.int32),
        "recv_rows": place_ends(jax.random.randint(seeds[9], (PARTS_X, PARTS_Y, 4, K), 0, E_DEV), jax.random.fold_in(seeds[9], 1), 0, E_DEV - 1).astype(jnp.int32),
        "move_src": draw_move_src(jax.random.fold_in(seeds[13], 71), 0),
        "move_dst": draw_move_dst(jax.random.fold_in(seeds[13], 71), 0),
        "move_slot": draw_move_slot(jax.random.fold_in(seeds[13], 71), 0),
    }


def product(left, right):
    return jnp.dot(left, right, precision=lax.Precision.HIGHEST, preferred_element_type=jnp.float32)


def reference(state, prop_base, prop_height, restrict, lift, layer_id, heights, degree, send_rows, recv_rows, move_src, move_dst, move_slot):
    count = PARTS_X * PARTS_Y
    flat_state = state.reshape(count * E_DEV, NB)
    offsets = (jnp.arange(count, dtype=jnp.int32) * E_DEV).reshape(PARTS_X, PARTS_Y, 1)
    send_index = (send_rows + offsets[..., None]).reshape(-1)
    recv_index = (recv_rows + offsets[..., None]).reshape(-1)
    flat_layer = layer_id.reshape(-1)
    tent_scale = heights.reshape(-1).astype(jnp.float32) / HMAX
    coeff = jnp.arange(NB, dtype=jnp.int32)
    coeff_mask = (coeff[None, :] < (NB * degree.reshape(-1) // PMAX)[:, None]).astype(jnp.float32)
    for layer_index in range(LAYERS):
        trace = product(flat_state[send_index], restrict).reshape(PARTS_X, PARTS_Y, 4, K, NT)
        zero_x = jnp.zeros((1, PARTS_Y, K, NT), jnp.float32)
        zero_y = jnp.zeros((PARTS_X, 1, K, NT), jnp.float32)
        from_minus_x = jnp.concatenate([zero_x, trace[:-1, :, 0]], axis=0)
        from_plus_x = jnp.concatenate([trace[1:, :, 1], zero_x], axis=0)
        from_minus_y = jnp.concatenate([zero_y, trace[:, :-1, 2]], axis=1)
        from_plus_y = jnp.concatenate([trace[:, 1:, 3], zero_y], axis=1)
        arriving = jnp.stack([from_minus_x, from_plus_x, from_minus_y, from_plus_y], axis=2)
        gathered = jnp.zeros((count * E_DEV, NT), jnp.float32).at[recv_index].add(arriving.reshape(-1, NT))
        inflow = product(gathered, lift)
        combined = flat_state + inflow
        advanced = coeff_mask * (product(combined, prop_base) + tent_scale[:, None] * product(combined, prop_height))
        flat_state = jnp.where((flat_layer <= layer_index)[:, None], advanced, flat_state)
    src_index = (move_src + offsets).reshape(-1)
    dst_index = (move_dst * E_DEV + move_slot).reshape(-1)
    result = flat_state.at[dst_index].set(flat_state[src_index])
    return result.reshape(PARTS_X, PARTS_Y, E_DEV, NB)
```

```python
import functools

import jax
import jax.numpy as jnp
from jax import lax
from jax.experimental import pallas as pl
from jax.experimental.pallas import tpu as pltpu
from jax.sharding import PartitionSpec as P

MESH = pl.DeviceIdType.MESH
F32 = jnp.float32
BF16 = jnp.bfloat16
LANES = 128
ROWS = 512


def split(value):
    high = value.astype(BF16)
    low = (value - high.astype(F32)).astype(BF16)
    return high, low


def pieces(value):
    high, low = split(value)
    return jnp.concatenate([high, low, high], axis=1)


def weights(value):
    high, low = split(value)
    return jnp.concatenate([high, high, low], axis=0)


def product(left, right):
    return jnp.dot(left, right, preferred_element_type=F32)


def column(row):
    return jnp.transpose(jnp.broadcast_to(row, (LANES, LANES)))


def gather_kernel(state, meta, send_idx, recv_idx, rows_out, rows_meta, recv_meta, all_meta, held, held_meta, sems, meta_sem):
    chunks = sems.shape[0]
    size = held.shape[0] // chunks
    for chunk in range(chunks):
        part = pl.ds(chunk * size, size)
        pltpu.make_async_copy(state.at[part], held.at[part], sems.at[chunk]).start()

    def spread(block, carry):
        held_meta[pl.ds(pl.multiple_of(block * LANES, LANES), LANES), :] = column(meta[pl.ds(block, 1), :])
        return carry

    lax.fori_loop(0, meta.shape[0], spread, 0)
    out_copy = pltpu.make_async_copy(held_meta, all_meta, meta_sem)
    out_copy.start()

    def take_meta(step, carry):
        first = pl.multiple_of(step * 16, 16)
        for lane in range(16):
            row = recv_idx[first + lane]
            recv_meta[pl.ds(first + lane, 1), :] = held_meta[pl.ds(row, 1), :]
        return carry

    lax.fori_loop(0, recv_meta.shape[0] // 16, take_meta, 0)
    for chunk in range(chunks):
        part = pl.ds(chunk * size, size)
        pltpu.make_async_copy(state.at[part], held.at[part], sems.at[chunk]).wait()

    def take(step, carry):
        first = pl.multiple_of(step * 16, 16)
        for lane in range(16):
            row = send_idx[first + lane]
            rows_out[pl.ds(first + lane, 1), :] = held[pl.ds(row, 1), :]
            rows_meta[pl.ds(first + lane, 1), :] = held_meta[pl.ds(row, 1), :]
        return carry

    lax.fori_loop(0, rows_out.shape[0] // 16, take, 0)
    out_copy.wait()


def layers_kernel(
    parts_x,
    parts_y,
    layers,
    windows,
    state,
    all_meta,
    rows_in,
    rows_meta,
    recv_meta,
    send_ids,
    recv_ids,
    slots,
    base,
    height,
    restrict,
    lift,
    bulk_out,
    correction,
    moved_out,
    slots_out,
    rows,
    held,
    held_meta,
    match,
    trace,
    arrived,
    arrived_pieces,
    prop_w,
    restrict_w,
    lift_w,
    move_out,
    move_in,
    slot_in,
    send_sem,
    recv_sem,
    state_sem,
    meta_sem,
    bulk_sem,
    slot_send,
    slot_recv,
    move_send,
    move_recv,
):
    px, py = lax.axis_index("px"), lax.axis_index("py")
    parts = parts_x * parts_y
    me = px * parts_y + py
    width = rows.shape[1]
    sent = trace.shape[1]
    side = sent // 4
    moves = rows.shape[0] - sent
    blocks = held.shape[0] // ROWS

    barrier = pltpu.get_barrier_semaphore()

    def greet(step, carry):
        other = lax.rem(me + step, parts)
        pl.semaphore_signal(barrier, inc=1, device_id=(other // parts_y, lax.rem(other, parts_y)), device_id_type=MESH)
        return carry

    lax.fori_loop(1, parts, greet, 0)

    def block_of(ref, block):
        return ref.at[pl.ds(pl.multiple_of(block * ROWS, ROWS), ROWS)]

    state_in = [
        pltpu.make_async_copy(state, held, state_sem),
        pltpu.make_async_copy(all_meta, held_meta, meta_sem),
    ]
    for copy in state_in:
        copy.start()

    def neighbour(side_index):
        dx = jnp.where(side_index == 0, 1, jnp.where(side_index == 1, -1, 0))
        dy = jnp.where(side_index == 2, 1, jnp.where(side_index == 3, -1, 0))
        x, y = px + dx, py + dy
        exists = (x >= 0) & (x < parts_x) & (y >= 0) & (y < parts_y)
        return x, y, exists

    def source_exists(side_index):
        dx = jnp.where(side_index == 0, -1, jnp.where(side_index == 1, 1, 0))
        dy = jnp.where(side_index == 2, -1, jnp.where(side_index == 3, 1, 0))
        x, y = px + dx, py + dy
        return (x >= 0) & (x < parts_x) & (y >= 0) & (y < parts_y)

    def trace_copy(layer, side_index, x, y):
        part = pl.ds(pl.multiple_of(side_index * side, side), side)
        return pltpu.make_async_remote_copy(
            src_ref=trace.at[layer, part],
            dst_ref=arrived.at[layer, part],
            send_sem=send_sem.at[layer, side_index],
            recv_sem=recv_sem.at[layer, side_index],
            device_id=(x, y),
            device_id_type=MESH,
        )

    def send_side(layer, side_index):
        x, y, exists = neighbour(side_index)

        @pl.when(exists)
        def _():
            trace_copy(layer, side_index, x, y).start()

    restrict_w[...] = weights(restrict[...])

    def first_trace(side_index, carry):
        part = pl.ds(pl.multiple_of(side_index * side, side), side)
        own = rows_in[part, :]
        rows[part, :] = own
        trace[0, part, :] = product(pieces(own), restrict_w[...])
        return carry

    lax.fori_loop(0, 4, first_trace, 0)
    pl.semaphore_wait(barrier, parts - 1)
    for side_index in range(4):
        send_side(0, side_index)

    def slot_copy(other):
        return pltpu.make_async_remote_copy(
            src_ref=slots.at[other],
            dst_ref=slot_in.at[me],
            send_sem=slot_send,
            recv_sem=slot_recv,
            device_id=(other // parts_y, lax.rem(other, parts_y)),
            device_id_type=MESH,
        )

    def move_copy(other):
        return pltpu.make_async_remote_copy(
            src_ref=move_out.at[other],
            dst_ref=move_in.at[me],
            send_sem=move_send,
            recv_sem=move_recv,
            device_id=(other // parts_y, lax.rem(other, parts_y)),
            device_id_type=MESH,
        )

    def send_slots(step, carry):
        slot_copy(lax.rem(me + step, parts)).start()
        return carry

    lax.fori_loop(1, parts, send_slots, 0)
    slot_in[pl.ds(me, 1)] = jnp.full((1, 1, LANES), held.shape[0], jnp.int32)
    move_in[pl.ds(me, 1)] = jnp.zeros((1, 4, LANES), F32)

    for side_index in range(4):

        @pl.when(jnp.logical_not(source_exists(side_index)))
        def _():
            for layer in range(layers):
                arrived[layer, pl.ds(side_index * side, side), :] = jnp.zeros((side, LANES), F32)

    rows[pl.ds(sent, moves), :] = rows_in[pl.ds(sent, moves), :]
    correction[...] = jnp.zeros_like(correction)
    prop_w[:, pl.ds(0, width)] = weights(base[...])
    prop_w[:, pl.ds(width, width)] = weights(height[...])
    lift_w[...] = weights(lift[...])

    def build_match(block, carry):
        ids = column(send_ids[pl.ds(block, 1), :])
        part = pl.ds(pl.multiple_of(block * LANES, LANES), LANES)
        for group in range(sent // LANES):
            same = ids == recv_ids[pl.ds(group, 1), :]
            match[part, pl.ds(group * LANES, LANES)] = jnp.where(same, 1.0, 0.0).astype(BF16)
        return carry

    lax.fori_loop(0, rows.shape[0] // LANES, build_match, 0)

    def advance(old, combined, meta, layer):
        both = product(pieces(combined), prop_w[...])
        scale = ((meta >> 2) & 7).astype(F32) * 0.25
        active = (meta >> 5) * (width // 4)
        pitched = (meta & 3) <= layer
        lane = lax.broadcasted_iota(jnp.int32, meta.shape, 1)
        halves = []
        for start in range(0, width, LANES):
            value = both[:, start : start + LANES] + scale * both[:, width + start : width + start + LANES]
            value = jnp.where(lane + start < active, value, 0.0)
            halves.append(jnp.where(pitched, value, old[:, start : start + LANES]))
        return jnp.concatenate(halves, axis=1)

    def bulk_copy(block):
        return pltpu.make_async_copy(block_of(held, block), block_of(bulk_out, block), bulk_sem.at[block])

    def bulk_block(block, carry):
        part = pl.ds(pl.multiple_of(block * ROWS, ROWS), ROWS)
        meta = held_meta[part, :]

        def one(layer, value):
            value = held[part, :]
            held[part, :] = advance(value, value, meta, layer)
            return 0

        lax.fori_loop(0, layers, one, 0)
        bulk_copy(block).start()
        return carry

    for copy in state_in:
        copy.wait()

    def compact(part, layer):
        match_rows = match[part, :]
        inflow = product(match_rows, arrived_pieces[...])
        inflow = inflow[:, :LANES] + inflow[:, LANES:]
        lifted = product(pieces(inflow), lift_w[...])
        old = rows[part, :]
        new = advance(old, old + lifted, rows_meta[part, :], layer)
        rows[part, :] = new
        return new

    def layer_step(layer, carry):
        first = jnp.where(layer == 0, 0, jnp.where(layer == 1, windows[0], windows[1]))
        last = jnp.where(layer == 0, windows[0], jnp.where(layer == 1, windows[1], windows[2]))
        lax.fori_loop(first, last, bulk_block, 0)
        for side_index in range(4):

            @pl.when(source_exists(side_index))
            def _():
                trace_copy(layer, side_index, px, py).wait_recv()

        def cut(side_index, carry):
            part = pl.ds(pl.multiple_of(side_index * side, side), side)
            high, low = split(arrived[layer, part, :])
            arrived_pieces[part, pl.ds(0, LANES)] = high
            arrived_pieces[part, pl.ds(LANES, LANES)] = low
            return carry

        lax.fori_loop(0, 4, cut, 0)

        @pl.when(layer < layers - 1)
        def _():
            def one_side(side_index, carry):
                part = pl.ds(pl.multiple_of(side_index * side, side), side)
                new = compact(part, layer)
                trace[layer + 1, part, :] = product(pieces(new), restrict_w[...])
                send_side(layer + 1, side_index)
                return carry

            lax.fori_loop(0, 4, one_side, 0)

        leaving = compact(pl.ds(sent, moves), layer)

        @pl.when(layer == layers - 1)
        def _():
            for place in range(2):
                for half in range(2):
                    move_out[:, 2 * place + half, :] = leaving[
                        place * parts : (place + 1) * parts, half * LANES : (half + 1) * LANES
                    ]

            def send_moves(step, carry):
                move_copy(lax.rem(me + step, parts)).start()
                return carry

            lax.fori_loop(1, parts, send_moves, 0)

        def correct(side_index, carry):
            part = pl.ds(pl.multiple_of(side_index * side, side), side)
            high = arrived_pieces[part, pl.ds(0, LANES)]
            low = arrived_pieces[part, pl.ds(LANES, LANES)]
            lifted = product(jnp.concatenate([high, low, high], axis=1), lift_w[...])
            old = correction[part, :]
            correction[part, :] = advance(old, old + lifted, recv_meta[part, :], layer)
            return carry

        lax.fori_loop(0, 4, correct, 0)
        return carry

    lax.fori_loop(0, layers, layer_step, 0)
    lax.fori_loop(windows[2], blocks, bulk_block, 0)

    def finish_bulk(block, carry):
        bulk_copy(block).wait()
        return carry

    lax.fori_loop(0, blocks, finish_bulk, 0)
    for side_index in range(4):
        x, y, exists = neighbour(side_index)

        @pl.when(exists)
        def _():
            for layer in range(layers):
                trace_copy(layer, side_index, x, y).wait_send()

    def whole(src, dst, sends, receives):
        return pltpu.make_async_remote_copy(
            src_ref=src.at[pl.ds(0, parts - 1)],
            dst_ref=dst.at[pl.ds(0, parts - 1)],
            send_sem=sends,
            recv_sem=receives,
            device_id=(px, py),
            device_id_type=MESH,
        )

    whole(slots, slot_in, slot_send, slot_recv).wait()
    whole(move_out, move_in, move_send, move_recv).wait()
    moved_out[...] = move_in[...]
    slots_out[...] = slot_in[...]


def scatter_kernel(bulk, correction, moved, recv_idx, repeats, slots, out, held, sems, out_sems):
    chunks = sems.shape[0]
    count = out.shape[0]
    size = count // chunks
    width = out.shape[1]
    for chunk in range(chunks):
        part = pl.ds(chunk * size, size)
        pltpu.make_async_copy(bulk.at[part], held.at[part], sems.at[chunk]).start()
    for chunk in range(chunks):
        part = pl.ds(chunk * size, size)
        pltpu.make_async_copy(bulk.at[part], held.at[part], sems.at[chunk]).wait()

    def add(step, carry):
        first = pl.multiple_of(step * 8, 8)

        @pl.when(repeats[step] == 0)
        def _():
            rows = [recv_idx[first + lane] for lane in range(8)]
            sums = [held[pl.ds(row, 1), :] + correction[pl.ds(first + lane, 1), :] for lane, row in enumerate(rows)]
            for row, value in zip(rows, sums):
                held[pl.ds(row, 1), :] = value

        @pl.when(repeats[step] != 0)
        def _():
            for lane in range(8):
                row = recv_idx[first + lane]
                held[pl.ds(row, 1), :] = held[pl.ds(row, 1), :] + correction[pl.ds(first + lane, 1), :]

        return carry

    lax.fori_loop(0, correction.shape[0] // 8, add, 0)

    def land(step, carry):
        for inner in range(4):
            source = step * 4 + inner
            for place in range(2):
                row = slots[source * 2 + place]
                halves = [moved[source, pl.ds(2 * place + half, 1), :] for half in range(width // LANES)]
                held[pl.ds(row, 1), :] = jnp.concatenate(halves, axis=1)
        return carry

    lax.fori_loop(0, moved.shape[0] // 4, land, 0)
    for chunk in range(chunks):
        part = pl.ds(chunk * size, size)
        pltpu.make_async_copy(held.at[part], out.at[part], out_sems.at[chunk]).start()
    for chunk in range(chunks):
        part = pl.ds(chunk * size, size)
        pltpu.make_async_copy(held.at[part], out.at[part], out_sems.at[chunk]).wait()


VMEM = pl.BlockSpec(memory_space=pltpu.VMEM)
SMEM = pl.BlockSpec(memory_space=pltpu.SMEM)
ANY = pl.BlockSpec(memory_space=pl.ANY)
LIMIT = 60 * 1024 * 1024


def local(
    state,
    prop_base,
    prop_height,
    restrict,
    lift,
    layer_id,
    heights,
    degree,
    send_rows,
    recv_rows,
    move_src,
    move_dst,
    move_slot,
):
    parts_x, parts_y = lax.axis_size("px"), lax.axis_size("py")
    parts = parts_x * parts_y
    current = state[0, 0]
    count, width = current.shape
    layers = 3
    recv_list = recv_rows[0, 0].reshape(-1)
    sent = recv_list.shape[0]
    moves = 2 * parts
    meta = (layer_id[0, 0] + 4 * heights[0, 0] + 32 * degree[0, 0]).astype(F32).reshape(-1, LANES)
    meta = meta.astype(jnp.int32)

    target, leaving, landing = move_dst[0, 0], move_src[0, 0], move_slot[0, 0]
    items = target.shape[0]
    order = lax.broadcasted_iota(jnp.int32, (items, items), 1) < lax.broadcasted_iota(jnp.int32, (items, items), 0)
    place = jnp.sum(((target[:, None] == target[None, :]) & order).astype(jnp.int32), axis=1)
    key = place * parts + target
    chosen = lax.broadcasted_iota(jnp.int32, (moves, items), 0) == key[None, :]
    move_idx = jnp.sum(jnp.where(chosen, leaving[None, :], 0), axis=1)
    move_to = count + jnp.sum(jnp.where(chosen, landing[None, :] - count, 0), axis=1)
    slots = jnp.pad(move_to.reshape(2, parts).T, ((0, 0), (0, LANES - 2)))[:, None, :]
    send_idx = jnp.concatenate([send_rows[0, 0].reshape(-1), move_idx])
    total = sent + moves

    rows, rows_meta, recv_meta, all_meta = pl.pallas_call(
        gather_kernel,
        name="gather_rows",
        out_shape=(
            jax.ShapeDtypeStruct((total, width), F32),
            jax.ShapeDtypeStruct((total, LANES), jnp.int32),
            jax.ShapeDtypeStruct((sent, LANES), jnp.int32),
            jax.ShapeDtypeStruct((count, LANES), jnp.int32),
        ),
        in_specs=[ANY, VMEM, SMEM, SMEM],
        out_specs=(VMEM, VMEM, VMEM, ANY),
        scratch_shapes=[
            pltpu.VMEM((count, width), F32),
            pltpu.VMEM((count, LANES), jnp.int32),
            pltpu.SemaphoreType.DMA((4,)),
            pltpu.SemaphoreType.DMA,
        ],
        compiler_params=pltpu.CompilerParams(vmem_limit_bytes=LIMIT),
    )(current, meta, send_idx, recv_list)

    blocks = count // ROWS
    windows = (blocks * 5 // 16, blocks * 9 // 16, blocks * 13 // 16)
    bulk, correction, moved, slots_in = pl.pallas_call(
        functools.partial(layers_kernel, parts_x, parts_y, layers, windows),
        name="layers",
        out_shape=(
            jax.ShapeDtypeStruct((count, width), F32),
            jax.ShapeDtypeStruct((sent, width), F32),
            jax.ShapeDtypeStruct((parts, 4, LANES), F32),
            jax.ShapeDtypeStruct((parts, 1, LANES), jnp.int32),
        ),
        in_specs=[ANY, ANY] + [VMEM] * 10,
        out_specs=(ANY, VMEM, VMEM, VMEM),
        scratch_shapes=[
            pltpu.VMEM((total, width), F32),
            pltpu.VMEM((count, width), F32),
            pltpu.VMEM((count, LANES), jnp.int32),
            pltpu.VMEM((total, sent), BF16),
            pltpu.VMEM((layers, sent, LANES), F32),
            pltpu.VMEM((layers, sent, LANES), F32),
            pltpu.VMEM((sent, 2 * LANES), BF16),
            pltpu.VMEM((3 * width, 2 * width), BF16),
            pltpu.VMEM((3 * width, LANES), BF16),
            pltpu.VMEM((3 * LANES, width), BF16),
            pltpu.VMEM((parts, 4, LANES), F32),
            pltpu.VMEM((parts, 4, LANES), F32),
            pltpu.VMEM((parts, 1, LANES), jnp.int32),
            pltpu.SemaphoreType.DMA((layers, 4)),
            pltpu.SemaphoreType.DMA((layers, 4)),
            pltpu.SemaphoreType.DMA,
            pltpu.SemaphoreType.DMA,
            pltpu.SemaphoreType.DMA((blocks,)),
            pltpu.SemaphoreType.DMA,
            pltpu.SemaphoreType.DMA,
            pltpu.SemaphoreType.DMA,
            pltpu.SemaphoreType.DMA,
        ],
        compiler_params=pltpu.CompilerParams(vmem_limit_bytes=LIMIT, collective_id=0, has_side_effects=True),
    )(
        current,
        all_meta,
        rows,
        rows_meta,
        recv_meta,
        send_idx.astype(F32).reshape(-1, LANES),
        recv_list.astype(F32).reshape(-1, LANES),
        slots,
        prop_base,
        prop_height,
        restrict,
        lift,
    )

    groups = recv_list.reshape(-1, 8)
    twins = jnp.sum((groups[:, :, None] == groups[:, None, :]).astype(jnp.int32), axis=(1, 2))
    repeats = (twins > 8).astype(jnp.int32)
    result = pl.pallas_call(
        scatter_kernel,
        name="scatter_rows",
        out_shape=jax.ShapeDtypeStruct((count, width), F32),
        in_specs=[ANY, VMEM, VMEM, SMEM, SMEM, SMEM],
        out_specs=ANY,
        scratch_shapes=[
            pltpu.VMEM((count + 8, width), F32),
            pltpu.SemaphoreType.DMA((4,)),
            pltpu.SemaphoreType.DMA((4,)),
        ],
        compiler_params=pltpu.CompilerParams(vmem_limit_bytes=LIMIT),
    )(bulk, correction, moved, recv_list, repeats, slots_in[:, 0, :2].reshape(-1))
    return result[None, None]


def solution(mesh):
    in_specs = (
        P("px", "py", None, None),
        P(),
        P(),
        P(),
        P(),
        P("px", "py", None),
        P("px", "py", None),
        P("px", "py", None),
        P("px", "py", None, None),
        P("px", "py", None, None),
        P("px", "py", None),
        P("px", "py", None),
        P("px", "py", None),
    )
    out_specs = P("px", "py", None, None)
    return jax.shard_map(local, mesh=mesh, in_specs=in_specs, out_specs=out_specs, check_vma=False)
```

```python
import functools

import jax
import jax.numpy as jnp
from jax import lax
from jax.experimental import pallas as pl
from jax.experimental.pallas import tpu as pltpu
from jax.sharding import PartitionSpec as P

MESH = pl.DeviceIdType.MESH
F32 = jnp.float32
BF16 = jnp.bfloat16
LANES = 128
ROWS = 1024
MARK = 1 << 20
BATCH = 16
PLACE_RECV = 24
SPARE = 8


def split(value):
    high = value.astype(BF16)
    return high, (value - high.astype(F32)).astype(BF16)


def pieces(values):
    pairs = [split(value) for value in values]
    high = [pair[0] for pair in pairs]
    return jnp.concatenate(high + [pair[1] for pair in pairs] + high, axis=1)


def weights(value):
    high, low = split(value)
    return jnp.concatenate([high, high, low], axis=0)


def product(left, right):
    return jnp.dot(left, right, preferred_element_type=F32)


def column(row):
    return jnp.transpose(jnp.broadcast_to(row, (LANES, LANES)))


def layers_kernel(
    parts_x,
    parts_y,
    layers,
    windows,
    state,
    meta,
    send_rows,
    recv_rows,
    target,
    leaving,
    landing,
    base,
    height,
    restrict,
    lift,
    bulk_out,
    correction_out,
    moved_out,
    slots_out,
    recv_out,
    rows,
    held,
    recv_meta,
    correction,
    match,
    trace,
    arrived,
    arrived_pieces,
    prop_w,
    restrict_w,
    lift_w,
    through_w,
    places,
    place_list,
    flat_ids,
    flat_recv,
    slots,
    move_out,
    move_in,
    slot_in,
    send_sem,
    recv_sem,
    state_sem,
    list_sem,
    bulk_sem,
    correction_sem,
    slot_send,
    slot_recv,
    move_send,
    move_recv,
):
    px, py = lax.axis_index("px"), lax.axis_index("py")
    parts = parts_x * parts_y
    me = px * parts_y + py
    count, width = state.shape[0] * 8, state.shape[2]
    sent = trace.shape[1]
    side = sent // 4
    moves = 2 * parts
    halves = width // LANES
    groups = halves + 1
    held_flat = held.reshape(held.shape[0] * 8 * groups, LANES)
    rows_flat = rows.reshape(rows.shape[0] * 8 * groups, LANES)
    blocks = count // ROWS
    chunks = state_sem.shape[0]

    barrier = pltpu.get_barrier_semaphore()

    def greet(step, carry):
        other = lax.rem(me + step, parts)
        pl.semaphore_signal(barrier, inc=1, device_id=(other // parts_y, lax.rem(other, parts_y)), device_id_type=MESH)
        return carry

    def state_copy(chunk, half):
        part = pl.ds(chunk * (count // 8 // chunks), count // 8 // chunks)
        return pltpu.make_async_copy(
            state.at[part, :, pl.ds(half * LANES, LANES)], held.at[part, half], state_sem.at[chunk, half]
        )

    for chunk in range(chunks):
        for half in range(halves):
            state_copy(chunk, half).start()
    lax.fori_loop(1, parts, greet, 0)

    def neighbour(side_index):
        dx = jnp.where(side_index == 0, 1, jnp.where(side_index == 1, -1, 0))
        dy = jnp.where(side_index == 2, 1, jnp.where(side_index == 3, -1, 0))
        x, y = px + dx, py + dy
        exists = (x >= 0) & (x < parts_x) & (y >= 0) & (y < parts_y)
        return x, y, exists

    def source_exists(side_index):
        dx = jnp.where(side_index == 0, -1, jnp.where(side_index == 1, 1, 0))
        dy = jnp.where(side_index == 2, -1, jnp.where(side_index == 3, 1, 0))
        x, y = px + dx, py + dy
        return (x >= 0) & (x < parts_x) & (y >= 0) & (y < parts_y)

    def trace_copy(layer, side_index, x, y):
        part = pl.ds(pl.multiple_of(side_index * side, side), side)
        return pltpu.make_async_remote_copy(
            src_ref=trace.at[layer, part],
            dst_ref=arrived.at[layer, part],
            send_sem=send_sem.at[layer, side_index],
            recv_sem=recv_sem.at[layer, side_index],
            device_id=(x, y),
            device_id_type=MESH,
        )

    def send_side(layer, side_index):
        x, y, exists = neighbour(side_index)

        @pl.when(exists)
        def _():
            trace_copy(layer, side_index, x, y).start()

    lane = lax.broadcasted_iota(jnp.int32, (LANES, LANES), 1)
    item = lax.broadcasted_iota(jnp.int32, (LANES, LANES), 0)
    to = column(target[...])
    earlier = (to == target[...]) & (item < lane)
    place = column(jnp.sum(jnp.where(earlier, 1, 0), axis=0, keepdims=True))
    source_of = column(leaving[...])
    landing_of = column(landing[...]) - count
    spread_slots = []
    for which in range(2):
        chosen = (to == lane) & (place == which)
        ids = jnp.sum(jnp.where(chosen, source_of, 0), axis=0, keepdims=True)
        flat_ids[pl.ds(sent // LANES + which, 1), :] = ids
        slot = count + jnp.sum(jnp.where(chosen, landing_of, 0), axis=0, keepdims=True)
        spread_slots.append(column(slot))
        flat_ids[pl.ds(sent // LANES + which, 1), :] = ids.astype(jnp.int32)
    for index in range(sent // LANES):
        side_index, start = index * LANES // side, index * LANES % side
        flat_ids[pl.ds(index, 1), :] = send_rows[side_index : side_index + 1, start : start + LANES]
        flat_recv[pl.ds(index, 1), :] = recv_rows[side_index : side_index + 1, start : start + LANES]
    places[pl.ds(0, flat_ids.shape[0]), :] = flat_ids[...] + (groups - 1) * 8 * (flat_ids[...] >> 3)
    received = flat_recv[...]
    places[pl.ds(PLACE_RECV, received.shape[0]), :] = received + (groups - 1) * 8 * (received >> 3)
    list_copy = pltpu.make_async_copy(places, place_list, list_sem)
    list_copy.start()
    slots[:, 0, :] = jnp.where(lane == 0, spread_slots[0], spread_slots[1])

    place_in_batch = lax.broadcasted_iota(jnp.int32, received.shape, 1) & (BATCH - 1)
    marks = jnp.zeros(received.shape, F32)
    for shift in range(1, BATCH):
        same = (received == pltpu.roll(received, shift, 1)) & (place_in_batch >= shift)
        marks = jnp.where(same, 1.0, marks)
    shift = 1
    while shift < BATCH:
        marks = jnp.maximum(marks, pltpu.roll(marks, shift, 1))
        shift *= 2
    spots = received + (halves - 1) * 8 * (received >> 3)
    recv_out[...] = spots + jnp.where((place_in_batch == BATCH - 1) & (marks > 0.5), MARK, 0)

    restrict_high, restrict_low = split(restrict[...])
    restrict_w[:, pl.ds(0, LANES)] = restrict_high
    restrict_w[:, pl.ds(LANES, LANES)] = restrict_low

    def spread(block, carry):
        part = pl.ds(pl.multiple_of(block * (LANES // 8), LANES // 8), LANES // 8)
        held[part, halves] = column(meta[pl.ds(block, 1), :]).reshape(LANES // 8, 8, LANES)
        return carry

    lax.fori_loop(0, meta.shape[0], spread, 0)

    def traced(values):
        pairs = [split(value) for value in values]
        high = jnp.concatenate([pair[0] for pair in pairs], axis=1)
        low = jnp.concatenate([pair[1] for pair in pairs], axis=1)
        both = product(high, restrict_w[...])
        return both[:, :LANES] + both[:, LANES:] + product(low, restrict_w[:, pl.ds(0, LANES)])

    def read(ref, first, size, which):
        part = pl.ds(pl.multiple_of(first // 8, size // 8), size // 8)
        return ref[part, which].reshape(size, LANES)

    def write(ref, first, size, values):
        part = pl.ds(pl.multiple_of(first // 8, size // 8), size // 8)
        for which, value in enumerate(values):
            ref[part, which] = value.reshape(size // 8, 8, LANES)

    def read_row(ref, first, size):
        return [read(ref, first, size, half) for half in range(halves)]

    list_copy.wait()
    for chunk in range(chunks):
        for half in range(halves):
            state_copy(chunk, half).wait()

    def take(line, carry):
        into = rows_flat.at[pl.ds(pl.multiple_of(line * (LANES * groups), LANES * groups), LANES * groups + SPARE * 8)]
        for inner in range(LANES):
            spot = inner // 8 * 8 * groups + inner % 8
            into[pl.ds(spot, groups, stride=8), :] = held_flat[pl.ds(place_list[line, inner], groups, stride=8), :]
        return carry

    for side_index in range(4):
        lax.fori_loop(side_index * (side // LANES), (side_index + 1) * (side // LANES), take, 0)
        trace[0, pl.ds(side_index * side, side), :] = traced(read_row(rows, side_index * side, side))
        if side_index == 0:
            pl.semaphore_wait(barrier, parts - 1)
        send_side(0, side_index)

    def slot_copy(other):
        return pltpu.make_async_remote_copy(
            src_ref=slots.at[other],
            dst_ref=slot_in.at[me],
            send_sem=slot_send,
            recv_sem=slot_recv,
            device_id=(other // parts_y, lax.rem(other, parts_y)),
            device_id_type=MESH,
        )

    def move_copy(other):
        return pltpu.make_async_remote_copy(
            src_ref=move_out.at[other],
            dst_ref=move_in.at[me],
            send_sem=move_send,
            recv_sem=move_recv,
            device_id=(other // parts_y, lax.rem(other, parts_y)),
            device_id_type=MESH,
        )

    def send_slots(step, carry):
        slot_copy(lax.rem(me + step, parts)).start()
        return carry

    lax.fori_loop(1, parts, send_slots, 0)
    slot_in[pl.ds(me, 1)] = jnp.full((1, 1, LANES), count, jnp.int32)
    move_in[pl.ds(me, 1)] = jnp.zeros((1, 4, LANES), F32)

    lax.fori_loop(sent // LANES, (sent + moves) // LANES, take, 0)

    def take_meta(line, carry):
        into = recv_meta.at[pl.ds(pl.multiple_of(line * LANES, LANES), LANES)]
        for inner in range(LANES):
            place = place_list[line + PLACE_RECV, inner]
            into[inner : inner + 1, :] = held_flat[pl.ds(place + 8 * halves, 1), :]
        return carry

    lax.fori_loop(0, sent // LANES, take_meta, 0)
    for side_index in range(4):

        @pl.when(jnp.logical_not(source_exists(side_index)))
        def _():
            for layer in range(layers):
                arrived[layer, pl.ds(side_index * side, side), :] = jnp.zeros((side, LANES), F32)

    prop_w[:, pl.ds(0, width)] = weights(base[...])
    prop_w[:, pl.ds(width, width)] = weights(height[...])
    lift_w[...] = weights(lift[...])
    through = product(pieces([lift[:, half * LANES : (half + 1) * LANES] for half in range(halves)]), prop_w[...])
    through_w[...] = weights(through)

    def match_rows_of(row, part):
        ids = column(row)
        for group in range(sent // LANES):
            same = ids == flat_recv[group : group + 1, :]
            match[part, pl.ds(group * LANES, LANES)] = jnp.where(same, 1.0, 0.0).astype(BF16)

    def build_match(block, carry):
        match_rows_of(flat_ids[pl.ds(block, 1), :], pl.ds(pl.multiple_of(block * LANES, LANES), LANES))
        return carry

    lax.fori_loop(0, (sent + moves) // LANES, build_match, 0)

    def finish(both, old, packed, layer):
        info = packed.astype(jnp.int32)
        scale = ((info >> 2) & 7).astype(F32) * 0.25
        active = (info >> 5) * (width // 4)
        pitched = (info & 3) <= layer
        lane = lax.broadcasted_iota(jnp.int32, info.shape, 1)
        values = []
        for half in range(halves):
            start = half * LANES
            value = both[:, start : start + LANES] + scale * both[:, width + start : width + start + LANES]
            value = jnp.where(lane + start < active, value, 0.0)
            values.append(jnp.where(pitched, value, 0.0 if old is None else old[half]))
        return values

    def advance(old, combined, packed, layer):
        return finish(product(pieces(combined), prop_w[...]), old, packed, layer)

    def bulk_copy(block):
        part = pl.ds(pl.multiple_of(block * (ROWS // 8), ROWS // 8), ROWS // 8)
        return pltpu.make_async_copy(held.at[part, pl.ds(0, halves)], bulk_out.at[part], bulk_sem.at[block])

    def bulk_block(block, carry):
        first = block * ROWS

        def one(layer, carry):
            values = read_row(held, first, ROWS)
            write(held, first, ROWS, advance(values, values, read(held, first, ROWS, halves), layer))
            return carry

        lax.fori_loop(0, layers, one, 0)
        bulk_copy(block).start()
        return carry

    def plus(values, added):
        return [value + added[:, half * LANES : (half + 1) * LANES] for half, value in enumerate(values)]

    def compact(first, size, layer):
        inflow = product(match[pl.ds(pl.multiple_of(first, size), size), :], arrived_pieces[...])
        lifted = product(pieces([inflow[:, :LANES] + inflow[:, LANES:]]), lift_w[...])
        old = read_row(rows, first, size)
        new = advance(old, plus(old, lifted), read(rows, first, size, halves), layer)
        write(rows, first, size, new)
        return new

    def correction_copy(side_index):
        part = pl.ds(pl.multiple_of(side_index * (side // 8), side // 8), side // 8)
        return pltpu.make_async_copy(correction.at[part], correction_out.at[part], correction_sem.at[side_index])

    def layer_step(layer, carry):
        first = jnp.where(layer == 0, 0, jnp.where(layer == 1, windows[0], windows[1]))
        last = jnp.where(layer == 0, windows[0], jnp.where(layer == 1, windows[1], windows[2]))
        lax.fori_loop(first, last, bulk_block, 0)
        for side_index in range(4):

            @pl.when(source_exists(side_index))
            def _():
                trace_copy(layer, side_index, px, py).wait_recv()

        def cut(side_index, carry):
            part = pl.ds(pl.multiple_of(side_index * side, side), side)
            high, low = split(arrived[layer, part, :])
            arrived_pieces[part, pl.ds(0, LANES)] = high
            arrived_pieces[part, pl.ds(LANES, LANES)] = low
            return carry

        lax.fori_loop(0, 4, cut, 0)

        @pl.when(layer < layers - 1)
        def _():
            def two_sides(pair, carry):
                part = pl.ds(pl.multiple_of(pair * 2 * side, 2 * side), 2 * side)
                trace[layer + 1, part, :] = traced(compact(pair * 2 * side, 2 * side, layer))
                send_side(layer + 1, 2 * pair)
                send_side(layer + 1, 2 * pair + 1)
                return carry

            lax.fori_loop(0, 2, two_sides, 0)

        leaving_rows = compact(sent, moves, layer)

        @pl.when(layer == layers - 1)
        def _():
            for which in range(2):
                for half in range(2):
                    move_out[:, 2 * which + half, :] = leaving_rows[half][which * parts : (which + 1) * parts]

            def send_moves(step, carry):
                move_copy(lax.rem(me + step, parts)).start()
                return carry

            lax.fori_loop(1, parts, send_moves, 0)

        def correct(pair, carry):
            part = pl.ds(pl.multiple_of(pair * 2 * side, 2 * side), 2 * side)
            high = arrived_pieces[part, pl.ds(0, LANES)]
            low = arrived_pieces[part, pl.ds(LANES, LANES)]
            triple = jnp.concatenate([high, low, high], axis=1)
            info = recv_meta[part, :]
            first = pair * 2 * side

            @pl.when(layer == 0)
            def _():
                write(correction, first, 2 * side, finish(product(triple, through_w[...]), None, info, layer))

            @pl.when(layer > 0)
            def _():
                old = read_row(correction, first, 2 * side)
                new = advance(old, plus(old, product(triple, lift_w[...])), info, layer)
                write(correction, first, 2 * side, new)

            @pl.when(layer == layers - 1)
            def _():
                correction_copy(2 * pair).start()
                correction_copy(2 * pair + 1).start()

            return carry

        lax.fori_loop(0, 2, correct, 0)
        return carry

    lax.fori_loop(0, layers, layer_step, 0)
    lax.fori_loop(windows[2], blocks, bulk_block, 0)

    def whole(src, dst, sends, receives):
        return pltpu.make_async_remote_copy(
            src_ref=src.at[pl.ds(0, parts - 1)],
            dst_ref=dst.at[pl.ds(0, parts - 1)],
            send_sem=sends,
            recv_sem=receives,
            device_id=(px, py),
            device_id_type=MESH,
        )

    whole(slots, slot_in, slot_send, slot_recv).wait()
    landed = jnp.transpose(slot_in[:, 0, :])[:2, :]
    slots_out[...] = landed + (halves - 1) * 8 * (landed >> 3)

    def finish_bulk(block, carry):
        bulk_copy(block).wait()
        return carry

    lax.fori_loop(0, blocks, finish_bulk, 0)
    for side_index in range(4):
        correction_copy(side_index).wait()
        x, y, exists = neighbour(side_index)

        @pl.when(exists)
        def _():
            for layer in range(layers):
                trace_copy(layer, side_index, x, y).wait_send()

    whole(move_out, move_in, move_send, move_recv).wait()
    moved_out[pl.ds(0, parts)] = move_in[...]


def scatter_kernel(bulk, correction, moved, recv_list, slots, out, held, added, sems, added_sem, out_sems):
    chunks = sems.shape[0]
    tiles, halves = bulk.shape[:2]
    size = tiles // chunks
    held_flat = held.reshape(held.shape[0] * halves * 8, LANES)
    added_flat = added.reshape(added.shape[0] * halves * 8, LANES)

    def bulk_copy(chunk):
        part = pl.ds(chunk * size, size)
        return pltpu.make_async_copy(bulk.at[part], held.at[part], sems.at[chunk])

    def out_copy(chunk, half):
        part = pl.ds(chunk * size, size)
        return pltpu.make_async_copy(
            held.at[part, half], out.at[part, :, pl.ds(half * LANES, LANES)], out_sems.at[chunk, half]
        )

    added_copy = pltpu.make_async_copy(correction, added.at[pl.ds(0, correction.shape[0])], added_sem)
    added_copy.start()
    for chunk in range(chunks):
        bulk_copy(chunk).start()
    added_copy.wait()
    for chunk in range(chunks):
        bulk_copy(chunk).wait()

    def add(line, carry):
        for batch in range(LANES // BATCH):
            first = pl.multiple_of((line * LANES + batch * BATCH) * halves, BATCH * halves)
            source = added_flat.at[pl.ds(first, BATCH * halves + SPARE * 8)]
            start = batch * BATCH
            last = recv_list[line, start + BATCH - 1]

            @pl.when(last < MARK)
            def _():
                spots = [recv_list[line, start + inner] for inner in range(BATCH)]
                sums = []
                for inner, spot in enumerate(spots):
                    own = source[pl.ds(inner // 8 * 8 * halves + inner % 8, halves, stride=8), :]
                    sums.append(held_flat[pl.ds(spot, halves, stride=8), :] + own)
                for spot, value in zip(spots, sums):
                    held_flat[pl.ds(spot, halves, stride=8), :] = value

            @pl.when(last >= MARK)
            def _():
                def one(inner, carry):
                    spot = recv_list[line, start + inner] & (MARK - 1)
                    own = added_flat[pl.ds(first + inner // 8 * 8 * halves + lax.rem(inner, 8), halves, stride=8), :]
                    held_flat[pl.ds(spot, halves, stride=8), :] = held_flat[pl.ds(spot, halves, stride=8), :] + own
                    return carry

                lax.fori_loop(0, BATCH, one, 0)

        return carry

    lax.fori_loop(0, recv_list.shape[0], add, 0)

    for which in range(2):
        for source in range(slots.shape[1]):
            spot = slots[which, source]
            held_flat[pl.ds(spot, halves, stride=8), :] = moved[source, pl.ds(halves * which, halves), :]
    for chunk in range(chunks):
        for half in range(halves):
            out_copy(chunk, half).start()
    for chunk in range(chunks):
        for half in range(halves):
            out_copy(chunk, half).wait()


VMEM = pl.BlockSpec(memory_space=pltpu.VMEM)
SMEM = pl.BlockSpec(memory_space=pltpu.SMEM)
ANY = pl.BlockSpec(memory_space=pl.ANY)
LIMIT = 60 * 1024 * 1024


def local(
    state,
    prop_base,
    prop_height,
    restrict,
    lift,
    layer_id,
    heights,
    degree,
    send_rows,
    recv_rows,
    move_src,
    move_dst,
    move_slot,
):
    parts_x, parts_y = lax.axis_size("px"), lax.axis_size("py")
    parts = parts_x * parts_y
    current = state[0, 0]
    count, width = current.shape
    halves = width // LANES
    layers = 3
    to_send, to_take = send_rows[0, 0], recv_rows[0, 0]
    sent = to_take.size
    total = sent + 2 * parts
    meta = (layer_id[0, 0] + 4 * heights[0, 0] + 32 * degree[0, 0]).astype(F32).reshape(-1, LANES)
    blocks = count // ROWS
    windows = (blocks // 8, blocks * 3 // 8, blocks * 5 // 8)
    bulk, correction, moved, slots, marked = pl.pallas_call(
        functools.partial(layers_kernel, parts_x, parts_y, layers, windows),
        name="layers",
        out_shape=(
            jax.ShapeDtypeStruct((count // 8, halves, 8, LANES), F32),
            jax.ShapeDtypeStruct((sent // 8, halves, 8, LANES), F32),
            jax.ShapeDtypeStruct((parts + SPARE, 4, LANES), F32),
            jax.ShapeDtypeStruct((2, parts), jnp.int32),
            jax.ShapeDtypeStruct((sent // LANES, LANES), jnp.int32),
        ),
        in_specs=[ANY] + [VMEM] * 10,
        out_specs=(ANY, ANY, VMEM, VMEM, VMEM),
        scratch_shapes=[
            pltpu.VMEM((total // 8 + SPARE, halves + 1, 8, LANES), F32),
            pltpu.VMEM((count // 8 + SPARE, halves + 1, 8, LANES), F32),
            pltpu.VMEM((sent + 8, LANES), F32),
            pltpu.VMEM((sent // 8, halves, 8, LANES), F32),
            pltpu.VMEM((total, sent), BF16),
            pltpu.VMEM((layers, sent, LANES), F32),
            pltpu.VMEM((layers, sent, LANES), F32),
            pltpu.VMEM((sent, 2 * LANES), BF16),
            pltpu.VMEM((3 * width, 2 * width), BF16),
            pltpu.VMEM((width, 2 * LANES), BF16),
            pltpu.VMEM((3 * LANES, width), BF16),
            pltpu.VMEM((3 * LANES, 2 * width), BF16),
            pltpu.VMEM((PLACE_RECV + sent // LANES, LANES), jnp.int32),
            pltpu.SMEM((PLACE_RECV + sent // LANES, LANES), jnp.int32),
            pltpu.VMEM((total // LANES, LANES), jnp.int32),
            pltpu.VMEM((sent // LANES, LANES), jnp.int32),
            pltpu.VMEM((parts, 1, LANES), jnp.int32),
            pltpu.VMEM((parts, 4, LANES), F32),
            pltpu.VMEM((parts, 4, LANES), F32),
            pltpu.VMEM((parts, 1, LANES), jnp.int32),
            pltpu.SemaphoreType.DMA((layers, 4)),
            pltpu.SemaphoreType.DMA((layers, 4)),
            pltpu.SemaphoreType.DMA((4, halves)),
            pltpu.SemaphoreType.DMA,
            pltpu.SemaphoreType.DMA((blocks,)),
            pltpu.SemaphoreType.DMA((4,)),
            pltpu.SemaphoreType.DMA,
            pltpu.SemaphoreType.DMA,
            pltpu.SemaphoreType.DMA,
            pltpu.SemaphoreType.DMA,
        ],
        compiler_params=pltpu.CompilerParams(vmem_limit_bytes=LIMIT, collective_id=0, has_side_effects=True),
    )(
        current.reshape(count // 8, 8, width),
        meta,
        to_send,
        to_take,
        move_dst[0],
        move_src[0],
        move_slot[0],
        prop_base,
        prop_height,
        restrict,
        lift,
    )
    result = pl.pallas_call(
        scatter_kernel,
        name="scatter_rows",
        out_shape=jax.ShapeDtypeStruct((count // 8, 8, width), F32),
        in_specs=[ANY, ANY, VMEM, SMEM, SMEM],
        out_specs=ANY,
        scratch_shapes=[
            pltpu.VMEM((count // 8 + 1 + SPARE, halves, 8, LANES), F32),
            pltpu.VMEM((sent // 8 + SPARE, halves, 8, LANES), F32),
            pltpu.SemaphoreType.DMA((4,)),
            pltpu.SemaphoreType.DMA,
            pltpu.SemaphoreType.DMA((4, halves)),
        ],
        compiler_params=pltpu.CompilerParams(vmem_limit_bytes=LIMIT),
    )(bulk, correction, moved, marked, slots)
    return result.reshape(count, width)[None, None]


def solution(mesh):
    in_specs = (
        P("px", "py", None, None),
        P(),
        P(),
        P(),
        P(),
        P("px", "py", None),
        P("px", "py", None),
        P("px", "py", None),
        P("px", "py", None, None),
        P("px", "py", None, None),
        P("px", "py", None),
        P("px", "py", None),
        P("px", "py", None),
    )
    out_specs = P("px", "py", None, None)
    return jax.shard_map(local, mesh=mesh, in_specs=in_specs, out_specs=out_specs, check_vma=False)
```

```python
import functools

import jax
import jax.numpy as jnp
from jax import lax
from jax.experimental import pallas as pl
from jax.experimental.pallas import tpu as pltpu
from jax.sharding import PartitionSpec as P

MESH = pl.DeviceIdType.MESH
F32 = jnp.float32
BF16 = jnp.bfloat16
LANES = 128
ROWS = 1024
MARK = 1 << 20
BATCH = 16
PLACE_RECV = 24
SPARE = 8


def split(value):
    high = value.astype(BF16)
    return high, (value - high.astype(F32)).astype(BF16)


def pieces(values):
    pairs = [split(value) for value in values]
    high = [pair[0] for pair in pairs]
    return jnp.concatenate(high + [pair[1] for pair in pairs] + high, axis=1)


def weights(value):
    high, low = split(value)
    return jnp.concatenate([high, high, low], axis=0)


def product(left, right):
    return jnp.dot(left, right, preferred_element_type=F32)


def column(row):
    return jnp.transpose(jnp.broadcast_to(row, (LANES, LANES)))


def layers_kernel(
    parts_x,
    parts_y,
    layers,
    windows,
    state,
    layer_id,
    heights,
    degree,
    send_rows,
    recv_rows,
    target,
    leaving,
    landing,
    base,
    height,
    restrict,
    lift,
    bulk_out,
    correction_out,
    moved_out,
    slots_out,
    recv_out,
    rows,
    held,
    recv_meta,
    correction,
    match,
    trace,
    arrived,
    arrived_pieces,
    prop_w,
    restrict_w,
    lift_w,
    through_w,
    places,
    place_list,
    flat_ids,
    flat_recv,
    slots,
    move_out,
    move_in,
    slot_in,
    send_sem,
    recv_sem,
    state_sem,
    list_sem,
    bulk_sem,
    correction_sem,
    slot_send,
    slot_recv,
    move_send,
    move_recv,
):
    px, py = lax.axis_index("px"), lax.axis_index("py")
    parts = parts_x * parts_y
    me = px * parts_y + py
    count, width = state.shape[0] * 8, state.shape[2]
    sent = arrived.shape[1]
    side = sent // 4
    moves = 2 * parts
    halves = width // LANES
    groups = halves + 1
    held_flat = held.reshape(held.shape[0] * 8 * groups, LANES)
    rows_flat = rows.reshape(rows.shape[0] * 8 * groups, LANES)
    blocks = count // ROWS
    chunks = state_sem.shape[0]

    barrier = pltpu.get_barrier_semaphore()

    def each_other(action):
        def at_x(dx, carry):
            x = px + dx
            x = jnp.where(x >= parts_x, x - parts_x, x)
            for dy in range(parts_y):
                y = py + dy
                action(x, jnp.where(y >= parts_y, y - parts_y, y))
            return carry

        lax.fori_loop(1, parts_x, at_x, 0)
        for dy in range(1, parts_y):
            y = py + dy
            action(px, jnp.where(y >= parts_y, y - parts_y, y))

    def greet(x, y):
        pl.semaphore_signal(barrier, inc=1, device_id=(x, y), device_id_type=MESH)

    def state_copy(chunk, half):
        part = pl.ds(chunk * (count // 8 // chunks), count // 8 // chunks)
        return pltpu.make_async_copy(
            state.at[part, :, pl.ds(half * LANES, LANES)], held.at[part, half], state_sem.at[chunk, half]
        )

    for chunk in range(chunks):
        for half in range(halves):
            state_copy(chunk, half).start()
    each_other(greet)

    def neighbour(side_index):
        dx = jnp.where(side_index == 0, 1, jnp.where(side_index == 1, -1, 0))
        dy = jnp.where(side_index == 2, 1, jnp.where(side_index == 3, -1, 0))
        x, y = px + dx, py + dy
        exists = (x >= 0) & (x < parts_x) & (y >= 0) & (y < parts_y)
        return x, y, exists

    def source_exists(side_index):
        dx = jnp.where(side_index == 0, -1, jnp.where(side_index == 1, 1, 0))
        dy = jnp.where(side_index == 2, -1, jnp.where(side_index == 3, 1, 0))
        x, y = px + dx, py + dy
        return (x >= 0) & (x < parts_x) & (y >= 0) & (y < parts_y)

    def trace_copy(layer, side_index, x, y):
        part = pl.ds(pl.multiple_of(side_index * side, side), side)
        return pltpu.make_async_remote_copy(
            src_ref=trace.at[layer, part],
            dst_ref=arrived.at[layer, part],
            send_sem=send_sem.at[layer, side_index],
            recv_sem=recv_sem.at[layer, side_index],
            device_id=(x, y),
            device_id_type=MESH,
        )

    def send_side(layer, side_index):
        x, y, exists = neighbour(side_index)

        @pl.when(exists)
        def _():
            trace_copy(layer, side_index, x, y).start()

    lane = lax.broadcasted_iota(jnp.int32, (LANES, LANES), 1)
    item = lax.broadcasted_iota(jnp.int32, (LANES, LANES), 0)
    to = column(target[...])
    earlier = (to == target[...]) & (item < lane)
    place = column(jnp.sum(jnp.where(earlier, 1, 0), axis=0, keepdims=True))
    source_of = column(leaving[...])
    landing_of = column(landing[...]) - count
    spread_slots = []
    for which in range(2):
        chosen = (to == lane) & (place == which)
        ids = jnp.sum(jnp.where(chosen, source_of, 0), axis=0, keepdims=True)
        flat_ids[pl.ds(sent // LANES + which, 1), :] = ids
        slot = count + jnp.sum(jnp.where(chosen, landing_of, 0), axis=0, keepdims=True)
        spread_slots.append(column(slot))
        flat_ids[pl.ds(sent // LANES + which, 1), :] = ids.astype(jnp.int32)
    for index in range(sent // LANES):
        side_index, start = index * LANES // side, index * LANES % side
        flat_ids[pl.ds(index, 1), :] = send_rows[side_index : side_index + 1, start : start + LANES]
        flat_recv[pl.ds(index, 1), :] = recv_rows[side_index : side_index + 1, start : start + LANES]
    places[pl.ds(0, flat_ids.shape[0]), :] = flat_ids[...] + (groups - 1) * 8 * (flat_ids[...] >> 3)
    received = flat_recv[...]
    places[pl.ds(PLACE_RECV, received.shape[0]), :] = received + (groups - 1) * 8 * (received >> 3)
    list_copy = pltpu.make_async_copy(places, place_list, list_sem)
    list_copy.start()
    slots[:, 0, :] = jnp.where(lane == 0, spread_slots[0], spread_slots[1])

    place_in_batch = lax.broadcasted_iota(jnp.int32, received.shape, 1) & (BATCH - 1)
    marks = jnp.zeros(received.shape, F32)
    for shift in range(1, BATCH):
        same = (received == pltpu.roll(received, shift, 1)) & (place_in_batch >= shift)
        marks = jnp.where(same, 1.0, marks)
    shift = 1
    while shift < BATCH:
        marks = jnp.maximum(marks, pltpu.roll(marks, shift, 1))
        shift *= 2
    spots = received + (halves - 1) * 8 * (received >> 3)
    recv_out[...] = spots + jnp.where((place_in_batch == BATCH - 1) & (marks > 0.5), MARK, 0)

    restrict_high, restrict_low = split(restrict[...])
    restrict_w[:, pl.ds(0, LANES)] = restrict_high
    restrict_w[:, pl.ds(LANES, LANES)] = restrict_low

    def spread(block, carry):
        part = pl.ds(pl.multiple_of(block * (LANES // 8), LANES // 8), LANES // 8)
        cols = pl.ds(pl.multiple_of(block * LANES, LANES), LANES)
        info = layer_id[:, cols] + 4 * heights[:, cols] + 32 * degree[:, cols]
        held[part, halves] = column(info.astype(F32)).reshape(LANES // 8, 8, LANES)
        return carry

    lax.fori_loop(0, count // LANES, spread, 0)

    def traced(values):
        pairs = [split(value) for value in values]
        high = jnp.concatenate([pair[0] for pair in pairs], axis=1)
        low = jnp.concatenate([pair[1] for pair in pairs], axis=1)
        both = product(high, restrict_w[...])
        return both[:, :LANES] + both[:, LANES:] + product(low, restrict_w[:, pl.ds(0, LANES)])

    def read(ref, first, size, which):
        part = pl.ds(pl.multiple_of(first // 8, LANES // 8), size // 8)
        return ref[part, which].reshape(size, LANES)

    def write(ref, first, size, values):
        part = pl.ds(pl.multiple_of(first // 8, LANES // 8), size // 8)
        for which, value in enumerate(values):
            ref[part, which] = value.reshape(size // 8, 8, LANES)

    def read_row(ref, first, size):
        return [read(ref, first, size, half) for half in range(halves)]

    list_copy.wait()
    for chunk in range(chunks):
        for half in range(halves):
            state_copy(chunk, half).wait()

    def take(line, carry):
        into = rows_flat.at[pl.ds(pl.multiple_of(line * (LANES * groups), LANES * groups), LANES * groups + SPARE * 8)]
        for inner in range(LANES):
            spot = inner // 8 * 8 * groups + inner % 8
            into[pl.ds(spot, groups, stride=8), :] = held_flat[pl.ds(place_list[line, inner], groups, stride=8), :]
        return carry

    for side_index in range(4):
        lax.fori_loop(side_index * (side // LANES), (side_index + 1) * (side // LANES), take, 0)
        trace[0, pl.ds(side_index * side, side), :] = traced(read_row(rows, side_index * side, side))

    prop_w[:, pl.ds(0, width)] = weights(base[...])
    prop_w[:, pl.ds(width, width)] = weights(height[...])
    lift_w[...] = weights(lift[...])
    through = product(pieces([lift[:, half * LANES : (half + 1) * LANES] for half in range(halves)]), prop_w[...])
    through_w[...] = weights(through)

    pl.semaphore_wait(barrier, parts - 1)
    for side_index in range(4):
        send_side(0, side_index)

    def slot_copy(x, y):
        return pltpu.make_async_remote_copy(
            src_ref=slots.at[x * parts_y + y],
            dst_ref=slot_in.at[me],
            send_sem=slot_send,
            recv_sem=slot_recv,
            device_id=(x, y),
            device_id_type=MESH,
        )

    def move_copy(x, y):
        return pltpu.make_async_remote_copy(
            src_ref=move_out.at[x * parts_y + y],
            dst_ref=move_in.at[me],
            send_sem=move_send,
            recv_sem=move_recv,
            device_id=(x, y),
            device_id_type=MESH,
        )

    each_other(lambda x, y: slot_copy(x, y).start())
    slot_in[pl.ds(me, 1)] = jnp.full((1, 1, LANES), count, jnp.int32)
    move_in[pl.ds(me, 1)] = jnp.zeros((1, 4, LANES), F32)

    lax.fori_loop(sent // LANES, (sent + moves) // LANES, take, 0)

    def take_meta(line, carry):
        into = recv_meta.at[pl.ds(pl.multiple_of(line * LANES, LANES), LANES)]
        for inner in range(LANES):
            place = place_list[line + PLACE_RECV, inner]
            into[inner : inner + 1, :] = held_flat[pl.ds(place + 8 * halves, 1), :]
        return carry

    lax.fori_loop(0, sent // LANES, take_meta, 0)
    for side_index in range(4):

        @pl.when(jnp.logical_not(source_exists(side_index)))
        def _():
            for layer in range(layers):
                arrived[layer, pl.ds(side_index * side, side), :] = jnp.zeros((side, LANES), F32)

    def match_rows_of(row, part):
        ids = column(row)
        for group in range(sent // LANES):
            same = ids == flat_recv[group : group + 1, :]
            match[part, pl.ds(group * LANES, LANES)] = jnp.where(same, 1.0, 0.0).astype(BF16)

    def build_match(block, carry):
        match_rows_of(flat_ids[pl.ds(block, 1), :], pl.ds(pl.multiple_of(block * LANES, LANES), LANES))
        return carry

    lax.fori_loop(0, (sent + moves) // LANES, build_match, 0)

    def finish(both, old, packed, layer):
        info = packed.astype(jnp.int32)
        scale = ((info >> 2) & 7).astype(F32) * 0.25
        active = (info >> 5) * (width // 4)
        pitched = (info & 3) <= layer
        lane = lax.broadcasted_iota(jnp.int32, info.shape, 1)
        values = []
        for half in range(halves):
            start = half * LANES
            value = both[:, start : start + LANES] + scale * both[:, width + start : width + start + LANES]
            value = jnp.where(lane + start < active, value, 0.0)
            values.append(jnp.where(pitched, value, 0.0 if old is None else old[half]))
        return values

    def advance(old, combined, packed, layer):
        return finish(product(pieces(combined), prop_w[...]), old, packed, layer)

    def bulk_copy(block):
        part = pl.ds(pl.multiple_of(block * (ROWS // 8), ROWS // 8), ROWS // 8)
        return pltpu.make_async_copy(held.at[part, pl.ds(0, halves)], bulk_out.at[part], bulk_sem.at[block])

    def bulk_block(block, carry):
        first = block * ROWS

        def one(layer, carry):
            values = read_row(held, first, ROWS)
            write(held, first, ROWS, advance(values, values, read(held, first, ROWS, halves), layer))
            return carry

        lax.fori_loop(0, layers, one, 0)
        bulk_copy(block).start()
        return carry

    def plus(values, added):
        return [value + added[:, half * LANES : (half + 1) * LANES] for half, value in enumerate(values)]

    def compact(first, size, layer):
        parts_of = -(-size // 512)
        step = size // parts_of
        inflows = []
        for index in range(parts_of):
            part = pl.ds(pl.multiple_of(first + index * step, LANES), step)
            inflow = product(match[part, :], arrived_pieces[...])
            inflows.append(inflow[:, :LANES] + inflow[:, LANES:])
        lifted = jnp.concatenate([product(pieces([inflow]), lift_w[...]) for inflow in inflows], axis=0)
        old = read_row(rows, first, size)
        new = advance(old, plus(old, lifted), read(rows, first, size, halves), layer)
        write(rows, first, size, new)
        return new

    def correction_copy(side_index):
        part = pl.ds(pl.multiple_of(side_index * (side // 8), side // 8), side // 8)
        return pltpu.make_async_copy(correction.at[part], correction_out.at[part], correction_sem.at[side_index])

    def layer_step(layer, carry):
        first = jnp.where(layer == 0, 0, jnp.where(layer == 1, windows[0], windows[1]))
        last = jnp.where(layer == 0, windows[0], jnp.where(layer == 1, windows[1], windows[2]))
        lax.fori_loop(first, last, bulk_block, 0)
        for side_index in range(4):

            @pl.when(source_exists(side_index))
            def _():
                trace_copy(layer, side_index, px, py).wait_recv()

        def cut(side_index, carry):
            part = pl.ds(pl.multiple_of(side_index * side, side), side)
            high, low = split(arrived[layer, part, :])
            arrived_pieces[part, pl.ds(0, LANES)] = high
            arrived_pieces[part, pl.ds(LANES, LANES)] = low
            return carry

        lax.fori_loop(0, 4, cut, 0)

        @pl.when(layer < layers - 1)
        def _():
            size = (sent + moves) // 2

            def two_sides(pair, carry):
                trace[layer + 1, pl.ds(pl.multiple_of(pair * size, LANES), size), :] = traced(
                    compact(pair * size, size, layer)
                )
                send_side(layer + 1, 2 * pair)
                send_side(layer + 1, 2 * pair + 1)
                return carry

            lax.fori_loop(0, 2, two_sides, 0)

        @pl.when(layer == layers - 1)
        def _():
            leaving_rows = compact(sent, moves, layer)
            for which in range(2):
                for half in range(halves):
                    move_out[:, halves * which + half, :] = leaving_rows[half][which * parts : (which + 1) * parts]
            each_other(lambda x, y: move_copy(x, y).start())

        def correct(pair, carry):
            part = pl.ds(pl.multiple_of(pair * 2 * side, 2 * side), 2 * side)
            high = arrived_pieces[part, pl.ds(0, LANES)]
            low = arrived_pieces[part, pl.ds(LANES, LANES)]
            triple = jnp.concatenate([high, low, high], axis=1)
            info = recv_meta[part, :]
            first = pair * 2 * side

            @pl.when(layer == 0)
            def _():
                write(correction, first, 2 * side, finish(product(triple, through_w[...]), None, info, layer))

            @pl.when(layer > 0)
            def _():
                old = read_row(correction, first, 2 * side)
                new = advance(old, plus(old, product(triple, lift_w[...])), info, layer)
                write(correction, first, 2 * side, new)

            @pl.when(layer == layers - 1)
            def _():
                correction_copy(2 * pair).start()
                correction_copy(2 * pair + 1).start()

            return carry

        lax.fori_loop(0, 2, correct, 0)
        return carry

    lax.fori_loop(0, layers, layer_step, 0)
    lax.fori_loop(windows[2], blocks, bulk_block, 0)

    def whole(src, dst, sends, receives):
        return pltpu.make_async_remote_copy(
            src_ref=src.at[pl.ds(0, parts - 1)],
            dst_ref=dst.at[pl.ds(0, parts - 1)],
            send_sem=sends,
            recv_sem=receives,
            device_id=(px, py),
            device_id_type=MESH,
        )

    whole(slots, slot_in, slot_send, slot_recv).wait()
    landed = jnp.transpose(slot_in[:, 0, :])[:2, :]
    slots_out[...] = landed + (halves - 1) * 8 * (landed >> 3)

    def finish_bulk(block, carry):
        bulk_copy(block).wait()
        return carry

    lax.fori_loop(0, blocks, finish_bulk, 0)
    for side_index in range(4):
        correction_copy(side_index).wait()
        x, y, exists = neighbour(side_index)

        @pl.when(exists)
        def _():
            for layer in range(layers):
                trace_copy(layer, side_index, x, y).wait_send()

    whole(move_out, move_in, move_send, move_recv).wait()
    moved_out[pl.ds(0, parts)] = move_in[...]


def scatter_kernel(bulk, correction, moved, recv_list, slots, out, held, added, sems, added_sem, out_sems):
    chunks = sems.shape[0]
    tiles, halves = bulk.shape[:2]
    size = tiles // chunks
    held_flat = held.reshape(held.shape[0] * halves * 8, LANES)
    added_flat = added.reshape(added.shape[0] * halves * 8, LANES)

    def bulk_copy(chunk):
        part = pl.ds(chunk * size, size)
        return pltpu.make_async_copy(bulk.at[part], held.at[part], sems.at[chunk])

    def out_copy(chunk, half):
        part = pl.ds(chunk * size, size)
        return pltpu.make_async_copy(
            held.at[part, half], out.at[part, :, pl.ds(half * LANES, LANES)], out_sems.at[chunk, half]
        )

    added_copy = pltpu.make_async_copy(correction, added.at[pl.ds(0, correction.shape[0])], added_sem)
    added_copy.start()
    for chunk in range(chunks):
        bulk_copy(chunk).start()
    added_copy.wait()
    for chunk in range(chunks):
        bulk_copy(chunk).wait()

    def add(line, carry):
        for batch in range(LANES // BATCH):
            first = pl.multiple_of((line * LANES + batch * BATCH) * halves, BATCH * halves)
            source = added_flat.at[pl.ds(first, BATCH * halves + SPARE * 8)]
            start = batch * BATCH
            last = recv_list[line, start + BATCH - 1]

            @pl.when(last < MARK)
            def _():
                spots = [recv_list[line, start + inner] for inner in range(BATCH)]
                sums = []
                for inner, spot in enumerate(spots):
                    own = source[pl.ds(inner // 8 * 8 * halves + inner % 8, halves, stride=8), :]
                    sums.append(held_flat[pl.ds(spot, halves, stride=8), :] + own)
                for spot, value in zip(spots, sums):
                    held_flat[pl.ds(spot, halves, stride=8), :] = value

            @pl.when(last >= MARK)
            def _():
                def one(inner, carry):
                    spot = recv_list[line, start + inner] & (MARK - 1)
                    own = added_flat[pl.ds(first + inner // 8 * 8 * halves + lax.rem(inner, 8), halves, stride=8), :]
                    held_flat[pl.ds(spot, halves, stride=8), :] = held_flat[pl.ds(spot, halves, stride=8), :] + own
                    return carry

                lax.fori_loop(0, BATCH, one, 0)

        return carry

    lax.fori_loop(0, recv_list.shape[0], add, 0)

    for which in range(2):
        for source in range(slots.shape[1]):
            spot = slots[which, source]
            held_flat[pl.ds(spot, halves, stride=8), :] = moved[source, pl.ds(halves * which, halves), :]
    for chunk in range(chunks):
        for half in range(halves):
            out_copy(chunk, half).start()
    for chunk in range(chunks):
        for half in range(halves):
            out_copy(chunk, half).wait()


VMEM = pl.BlockSpec(memory_space=pltpu.VMEM)
SMEM = pl.BlockSpec(memory_space=pltpu.SMEM)
ANY = pl.BlockSpec(memory_space=pl.ANY)
LIMIT = 60 * 1024 * 1024


def local(
    state,
    prop_base,
    prop_height,
    restrict,
    lift,
    layer_id,
    heights,
    degree,
    send_rows,
    recv_rows,
    move_src,
    move_dst,
    move_slot,
):
    parts_x, parts_y = lax.axis_size("px"), lax.axis_size("py")
    parts = parts_x * parts_y
    current = state[0, 0]
    count, width = current.shape
    halves = width // LANES
    layers = 3
    to_send, to_take = send_rows[0, 0], recv_rows[0, 0]
    sent = to_take.size
    total = sent + 2 * parts
    blocks = count // ROWS
    windows = (blocks * 2 // 8, blocks * 4 // 8, blocks * 6 // 8)
    bulk, correction, moved, slots, marked = pl.pallas_call(
        functools.partial(layers_kernel, parts_x, parts_y, layers, windows),
        name="layers",
        out_shape=(
            jax.ShapeDtypeStruct((count // 8, halves, 8, LANES), F32),
            jax.ShapeDtypeStruct((sent // 8, halves, 8, LANES), F32),
            jax.ShapeDtypeStruct((parts + SPARE, 4, LANES), F32),
            jax.ShapeDtypeStruct((2, parts), jnp.int32),
            jax.ShapeDtypeStruct((sent // LANES, LANES), jnp.int32),
        ),
        in_specs=[ANY] + [VMEM] * 12,
        out_specs=(ANY, ANY, VMEM, VMEM, VMEM),
        scratch_shapes=[
            pltpu.VMEM((total // 8 + SPARE, halves + 1, 8, LANES), F32),
            pltpu.VMEM((count // 8 + SPARE, halves + 1, 8, LANES), F32),
            pltpu.VMEM((sent + 8, LANES), F32),
            pltpu.VMEM((sent // 8, halves, 8, LANES), F32),
            pltpu.VMEM((total, sent), BF16),
            pltpu.VMEM((layers, total, LANES), F32),
            pltpu.VMEM((layers, sent, LANES), F32),
            pltpu.VMEM((sent, 2 * LANES), BF16),
            pltpu.VMEM((3 * width, 2 * width), BF16),
            pltpu.VMEM((width, 2 * LANES), BF16),
            pltpu.VMEM((3 * LANES, width), BF16),
            pltpu.VMEM((3 * LANES, 2 * width), BF16),
            pltpu.VMEM((PLACE_RECV + sent // LANES, LANES), jnp.int32),
            pltpu.SMEM((PLACE_RECV + sent // LANES, LANES), jnp.int32),
            pltpu.VMEM((total // LANES, LANES), jnp.int32),
            pltpu.VMEM((sent // LANES, LANES), jnp.int32),
            pltpu.VMEM((parts, 1, LANES), jnp.int32),
            pltpu.VMEM((parts, 4, LANES), F32),
            pltpu.VMEM((parts, 4, LANES), F32),
            pltpu.VMEM((parts, 1, LANES), jnp.int32),
            pltpu.SemaphoreType.DMA((layers, 4)),
            pltpu.SemaphoreType.DMA((layers, 4)),
            pltpu.SemaphoreType.DMA((4, halves)),
            pltpu.SemaphoreType.DMA,
            pltpu.SemaphoreType.DMA((blocks,)),
            pltpu.SemaphoreType.DMA((4,)),
            pltpu.SemaphoreType.DMA,
            pltpu.SemaphoreType.DMA,
            pltpu.SemaphoreType.DMA,
            pltpu.SemaphoreType.DMA,
        ],
        compiler_params=pltpu.CompilerParams(vmem_limit_bytes=LIMIT, collective_id=0, has_side_effects=True),
    )(
        current.reshape(count // 8, 8, width),
        layer_id[0],
        heights[0],
        degree[0],
        to_send,
        to_take,
        move_dst[0],
        move_src[0],
        move_slot[0],
        prop_base,
        prop_height,
        restrict,
        lift,
    )
    result = pl.pallas_call(
        scatter_kernel,
        name="scatter_rows",
        out_shape=jax.ShapeDtypeStruct((count // 8, 8, width), F32),
        in_specs=[ANY, ANY, VMEM, SMEM, SMEM],
        out_specs=ANY,
        scratch_shapes=[
            pltpu.VMEM((count // 8 + 1 + SPARE, halves, 8, LANES), F32),
            pltpu.VMEM((sent // 8 + SPARE, halves, 8, LANES), F32),
            pltpu.SemaphoreType.DMA((4,)),
            pltpu.SemaphoreType.DMA,
            pltpu.SemaphoreType.DMA((4, halves)),
        ],
        compiler_params=pltpu.CompilerParams(vmem_limit_bytes=LIMIT),
    )(bulk, correction, moved, marked, slots)
    return result.reshape(count, width)[None, None]


def solution(mesh):
    in_specs = (
        P("px", "py", None, None),
        P(),
        P(),
        P(),
        P(),
        P("px", "py", None),
        P("px", "py", None),
        P("px", "py", None),
        P("px", "py", None, None),
        P("px", "py", None, None),
        P("px", "py", None),
        P("px", "py", None),
        P("px", "py", None),
    )
    out_specs = P("px", "py", None, None)
    return jax.shard_map(local, mesh=mesh, in_specs=in_specs, out_specs=out_specs, check_vma=False)
```

```python
import functools

import jax
import jax.numpy as jnp
from jax import lax
from jax.experimental import pallas as pl
from jax.experimental.pallas import tpu as pltpu
from jax.sharding import PartitionSpec as P

MESH = pl.DeviceIdType.MESH
F32 = jnp.float32
BF16 = jnp.bfloat16
LANES = 128
ROWS = 1024
MARK = 1 << 20
BATCH = 16
PLACE_RECV = 24
SPARE = 8


def split(value):
    high = value.astype(BF16)
    return high, (value - high.astype(F32)).astype(BF16)


def pieces(values):
    pairs = [split(value) for value in values]
    high = [pair[0] for pair in pairs]
    return jnp.concatenate(high + [pair[1] for pair in pairs] + high, axis=1)


def weights(value):
    high, low = split(value)
    return jnp.concatenate([high, high, low], axis=0)


def product(left, right):
    return jnp.dot(left, right, preferred_element_type=F32)


def column(row):
    return jnp.transpose(jnp.broadcast_to(row, (LANES, LANES)))


def layers_kernel(
    parts_x,
    parts_y,
    layers,
    windows,
    state,
    layer_id,
    heights,
    degree,
    send_rows,
    recv_rows,
    target,
    leaving,
    landing,
    base,
    height,
    restrict,
    lift,
    bulk_out,
    correction_out,
    moved_out,
    slots_out,
    recv_out,
    rows,
    held,
    recv_meta,
    correction,
    match,
    trace,
    arrived,
    arrived_pieces,
    prop_w,
    restrict_w,
    lift_w,
    through_w,
    places,
    place_list,
    flat_ids,
    flat_recv,
    slots,
    move_out,
    move_in,
    slot_in,
    send_sem,
    recv_sem,
    state_sem,
    list_sem,
    bulk_sem,
    correction_sem,
    slot_send,
    slot_recv,
    move_send,
    move_recv,
):
    px, py = lax.axis_index("px"), lax.axis_index("py")
    parts = parts_x * parts_y
    me = px * parts_y + py
    count, width = state.shape[0] * 8, state.shape[2]
    sent = arrived.shape[1]
    side = sent // 4
    moves = 2 * parts
    halves = width // LANES
    groups = halves + 1
    held_flat = held.reshape(held.shape[0] * 8 * groups, LANES)
    rows_flat = rows.reshape(rows.shape[0] * 8 * groups, LANES)
    blocks = count // ROWS
    chunks = state_sem.shape[0]

    barrier = pltpu.get_barrier_semaphore()

    def each_other(action):
        def at_x(dx, carry):
            x = px + dx
            x = jnp.where(x >= parts_x, x - parts_x, x)
            for dy in range(parts_y):
                y = py + dy
                action(x, jnp.where(y >= parts_y, y - parts_y, y))
            return carry

        lax.fori_loop(1, parts_x, at_x, 0)
        for dy in range(1, parts_y):
            y = py + dy
            action(px, jnp.where(y >= parts_y, y - parts_y, y))

    def greet(x, y):
        pl.semaphore_signal(barrier, inc=1, device_id=(x, y), device_id_type=MESH)

    def state_copy(chunk, half):
        part = pl.ds(chunk * (count // 8 // chunks), count // 8 // chunks)
        return pltpu.make_async_copy(
            state.at[part, :, pl.ds(half * LANES, LANES)], held.at[part, half], state_sem.at[chunk, half]
        )

    for chunk in range(chunks):
        for half in range(halves):
            state_copy(chunk, half).start()
    each_other(greet)

    def neighbour(side_index):
        dx = jnp.where(side_index == 0, 1, jnp.where(side_index == 1, -1, 0))
        dy = jnp.where(side_index == 2, 1, jnp.where(side_index == 3, -1, 0))
        x, y = px + dx, py + dy
        exists = (x >= 0) & (x < parts_x) & (y >= 0) & (y < parts_y)
        return x, y, exists

    def source_exists(side_index):
        dx = jnp.where(side_index == 0, -1, jnp.where(side_index == 1, 1, 0))
        dy = jnp.where(side_index == 2, -1, jnp.where(side_index == 3, 1, 0))
        x, y = px + dx, py + dy
        return (x >= 0) & (x < parts_x) & (y >= 0) & (y < parts_y)

    def trace_copy(layer, side_index, x, y):
        part = pl.ds(pl.multiple_of(side_index * side, side), side)
        return pltpu.make_async_remote_copy(
            src_ref=trace.at[layer, part],
            dst_ref=arrived.at[layer, part],
            send_sem=send_sem.at[layer, side_index],
            recv_sem=recv_sem.at[layer, side_index],
            device_id=(x, y),
            device_id_type=MESH,
        )

    def send_side(layer, side_index):
        x, y, exists = neighbour(side_index)

        @pl.when(exists)
        def _():
            trace_copy(layer, side_index, x, y).start()

    lane = lax.broadcasted_iota(jnp.int32, (LANES, LANES), 1)
    item = lax.broadcasted_iota(jnp.int32, (LANES, LANES), 0)
    to = column(target[...])
    earlier = (to == target[...]) & (item < lane)
    place = column(jnp.sum(jnp.where(earlier, 1, 0), axis=0, keepdims=True))
    source_of = column(leaving[...])
    landing_of = column(landing[...]) - count
    spread_slots = []
    for which in range(2):
        chosen = (to == lane) & (place == which)
        ids = jnp.sum(jnp.where(chosen, source_of, 0), axis=0, keepdims=True)
        flat_ids[pl.ds(sent // LANES + which, 1), :] = ids
        slot = count + jnp.sum(jnp.where(chosen, landing_of, 0), axis=0, keepdims=True)
        spread_slots.append(column(slot))
        flat_ids[pl.ds(sent // LANES + which, 1), :] = ids.astype(jnp.int32)
    for index in range(sent // LANES):
        side_index, start = index * LANES // side, index * LANES % side
        flat_ids[pl.ds(index, 1), :] = send_rows[side_index : side_index + 1, start : start + LANES]
        flat_recv[pl.ds(index, 1), :] = recv_rows[side_index : side_index + 1, start : start + LANES]
    places[pl.ds(0, flat_ids.shape[0]), :] = flat_ids[...] + (groups - 1) * 8 * (flat_ids[...] >> 3)
    received = flat_recv[...]
    places[pl.ds(PLACE_RECV, received.shape[0]), :] = received + (groups - 1) * 8 * (received >> 3)
    list_copy = pltpu.make_async_copy(places, place_list, list_sem)
    list_copy.start()
    slots[:, 0, :] = jnp.where(lane == 0, spread_slots[0], spread_slots[1])

    place_in_batch = lax.broadcasted_iota(jnp.int32, received.shape, 1) & (BATCH - 1)
    marks = jnp.zeros(received.shape, F32)
    for shift in range(1, BATCH):
        same = (received == pltpu.roll(received, shift, 1)) & (place_in_batch >= shift)
        marks = jnp.where(same, 1.0, marks)
    shift = 1
    while shift < BATCH:
        marks = jnp.maximum(marks, pltpu.roll(marks, shift, 1))
        shift *= 2
    spots = received + (halves - 1) * 8 * (received >> 3)
    recv_out[...] = spots + jnp.where((place_in_batch == BATCH - 1) & (marks > 0.5), MARK, 0)

    restrict_high, restrict_low = split(restrict[...])
    restrict_w[:, pl.ds(0, LANES)] = restrict_high
    restrict_w[:, pl.ds(LANES, LANES)] = restrict_low

    def spread(block, carry):
        part = pl.ds(pl.multiple_of(block * (LANES // 8), LANES // 8), LANES // 8)
        cols = pl.ds(pl.multiple_of(block * LANES, LANES), LANES)
        info = layer_id[:, cols] + 4 * heights[:, cols] + 32 * degree[:, cols]
        held[part, halves] = column(info.astype(F32)).reshape(LANES // 8, 8, LANES)
        return carry

    lax.fori_loop(0, count // LANES, spread, 0, unroll=4)

    def traced(values):
        pairs = [split(value) for value in values]
        high = jnp.concatenate([pair[0] for pair in pairs], axis=1)
        low = jnp.concatenate([pair[1] for pair in pairs], axis=1)
        both = product(high, restrict_w[...])
        return both[:, :LANES] + both[:, LANES:] + product(low, restrict_w[:, pl.ds(0, LANES)])

    def read(ref, first, size, which):
        part = pl.ds(pl.multiple_of(first // 8, LANES // 8), size // 8)
        return ref[part, which].reshape(size, LANES)

    def write(ref, first, size, values):
        part = pl.ds(pl.multiple_of(first // 8, LANES // 8), size // 8)
        for which, value in enumerate(values):
            ref[part, which] = value.reshape(size // 8, 8, LANES)

    def read_row(ref, first, size):
        return [read(ref, first, size, half) for half in range(halves)]

    list_copy.wait()
    for chunk in range(chunks):
        for half in range(halves):
            state_copy(chunk, half).wait()

    def take(line, carry):
        into = rows_flat.at[pl.ds(pl.multiple_of(line * (LANES * groups), LANES * groups), LANES * groups + SPARE * 8)]
        for inner in range(LANES):
            spot = inner // 8 * 8 * groups + inner % 8
            into[pl.ds(spot, groups, stride=8), :] = held_flat[pl.ds(place_list[line, inner], groups, stride=8), :]
        return carry

    for side_index in range(4):
        lax.fori_loop(side_index * (side // LANES), (side_index + 1) * (side // LANES), take, 0)
        trace[0, pl.ds(side_index * side, side), :] = traced(read_row(rows, side_index * side, side))

    prop_w[:, pl.ds(0, width)] = weights(base[...])
    prop_w[:, pl.ds(width, width)] = weights(height[...])
    lift_w[...] = weights(lift[...])
    through = product(pieces([lift[:, half * LANES : (half + 1) * LANES] for half in range(halves)]), prop_w[...])
    through_w[...] = weights(through)

    pl.semaphore_wait(barrier, parts - 1)
    for side_index in range(4):
        send_side(0, side_index)

    def slot_copy(x, y):
        return pltpu.make_async_remote_copy(
            src_ref=slots.at[x * parts_y + y],
            dst_ref=slot_in.at[me],
            send_sem=slot_send,
            recv_sem=slot_recv,
            device_id=(x, y),
            device_id_type=MESH,
        )

    def move_copy(x, y):
        return pltpu.make_async_remote_copy(
            src_ref=move_out.at[x * parts_y + y],
            dst_ref=move_in.at[me],
            send_sem=move_send,
            recv_sem=move_recv,
            device_id=(x, y),
            device_id_type=MESH,
        )

    each_other(lambda x, y: slot_copy(x, y).start())
    slot_in[pl.ds(me, 1)] = jnp.full((1, 1, LANES), count, jnp.int32)
    move_in[pl.ds(me, 1)] = jnp.zeros((1, 4, LANES), F32)

    lax.fori_loop(sent // LANES, (sent + moves) // LANES, take, 0)

    def take_meta(line, carry):
        into = recv_meta.at[pl.ds(pl.multiple_of(line * LANES, LANES), LANES)]
        for inner in range(LANES):
            place = place_list[line + PLACE_RECV, inner]
            into[inner : inner + 1, :] = held_flat[pl.ds(place + 8 * halves, 1), :]
        return carry

    lax.fori_loop(0, sent // LANES, take_meta, 0)
    for side_index in range(4):

        @pl.when(jnp.logical_not(source_exists(side_index)))
        def _():
            for layer in range(layers):
                arrived[layer, pl.ds(side_index * side, side), :] = jnp.zeros((side, LANES), F32)

    def match_rows_of(row, part):
        ids = column(row)
        for group in range(sent // LANES):
            same = ids == flat_recv[group : group + 1, :]
            match[part, pl.ds(group * LANES, LANES)] = jnp.where(same, 1.0, 0.0).astype(BF16)

    def build_match(block, carry):
        match_rows_of(flat_ids[pl.ds(block, 1), :], pl.ds(pl.multiple_of(block * LANES, LANES), LANES))
        return carry

    lax.fori_loop(0, (sent + moves) // LANES, build_match, 0)

    def finish(both, old, packed, layer):
        info = packed.astype(jnp.int32)
        scale = ((info >> 2) & 7).astype(F32) * 0.25
        active = (info >> 5) * (width // 4)
        pitched = (info & 3) <= layer
        lane = lax.broadcasted_iota(jnp.int32, info.shape, 1)
        values = []
        for half in range(halves):
            start = half * LANES
            value = both[:, start : start + LANES] + scale * both[:, width + start : width + start + LANES]
            value = jnp.where(lane + start < active, value, 0.0)
            values.append(jnp.where(pitched, value, 0.0 if old is None else old[half]))
        return values

    def advance(old, combined, packed, layer):
        return finish(product(pieces(combined), prop_w[...]), old, packed, layer)

    def bulk_copy(block):
        part = pl.ds(pl.multiple_of(block * (ROWS // 8), ROWS // 8), ROWS // 8)
        return pltpu.make_async_copy(held.at[part, pl.ds(0, halves)], bulk_out.at[part], bulk_sem.at[block])

    def bulk_block(block, carry):
        first = block * ROWS

        def one(layer, carry):
            values = read_row(held, first, ROWS)
            write(held, first, ROWS, advance(values, values, read(held, first, ROWS, halves), layer))
            return carry

        lax.fori_loop(0, layers, one, 0)
        bulk_copy(block).start()
        return carry

    def plus(values, added):
        return [value + added[:, half * LANES : (half + 1) * LANES] for half, value in enumerate(values)]

    def compact(first, size, layer):
        parts_of = -(-size // 512)
        step = size // parts_of
        inflows = []
        for index in range(parts_of):
            part = pl.ds(pl.multiple_of(first + index * step, LANES), step)
            inflow = product(match[part, :], arrived_pieces[...])
            inflows.append(inflow[:, :LANES] + inflow[:, LANES:])
        lifted = jnp.concatenate([product(pieces([inflow]), lift_w[...]) for inflow in inflows], axis=0)
        old = read_row(rows, first, size)
        new = advance(old, plus(old, lifted), read(rows, first, size, halves), layer)
        write(rows, first, size, new)
        return new

    def correction_copy(side_index):
        part = pl.ds(pl.multiple_of(side_index * (side // 8), side // 8), side // 8)
        return pltpu.make_async_copy(correction.at[part], correction_out.at[part], correction_sem.at[side_index])

    def layer_step(layer, carry):
        first = jnp.where(layer == 0, 0, jnp.where(layer == 1, windows[0], windows[1]))
        last = jnp.where(layer == 0, windows[0], jnp.where(layer == 1, windows[1], windows[2]))
        lax.fori_loop(first, last, bulk_block, 0)
        for side_index in range(4):

            @pl.when(source_exists(side_index))
            def _():
                trace_copy(layer, side_index, px, py).wait_recv()

        def cut(side_index, carry):
            part = pl.ds(pl.multiple_of(side_index * side, side), side)
            high, low = split(arrived[layer, part, :])
            arrived_pieces[part, pl.ds(0, LANES)] = high
            arrived_pieces[part, pl.ds(LANES, LANES)] = low
            return carry

        lax.fori_loop(0, 4, cut, 0)

        @pl.when(layer < layers - 1)
        def _():
            size = (sent + moves) // 2

            def two_sides(pair, carry):
                trace[layer + 1, pl.ds(pl.multiple_of(pair * size, LANES), size), :] = traced(
                    compact(pair * size, size, layer)
                )
                send_side(layer + 1, 2 * pair)
                send_side(layer + 1, 2 * pair + 1)
                return carry

            lax.fori_loop(0, 2, two_sides, 0)

        @pl.when(layer == layers - 1)
        def _():
            leaving_rows = compact(sent, moves, layer)
            for which in range(2):
                for half in range(halves):
                    move_out[:, halves * which + half, :] = leaving_rows[half][which * parts : (which + 1) * parts]
            each_other(lambda x, y: move_copy(x, y).start())

        def correct(pair, carry):
            part = pl.ds(pl.multiple_of(pair * 2 * side, 2 * side), 2 * side)
            high = arrived_pieces[part, pl.ds(0, LANES)]
            low = arrived_pieces[part, pl.ds(LANES, LANES)]
            triple = jnp.concatenate([high, low, high], axis=1)
            info = recv_meta[part, :]
            first = pair * 2 * side

            @pl.when(layer == 0)
            def _():
                write(correction, first, 2 * side, finish(product(triple, through_w[...]), None, info, layer))

            @pl.when(layer > 0)
            def _():
                old = read_row(correction, first, 2 * side)
                new = advance(old, plus(old, product(triple, lift_w[...])), info, layer)
                write(correction, first, 2 * side, new)

            @pl.when(layer == layers - 1)
            def _():
                correction_copy(2 * pair).start()
                correction_copy(2 * pair + 1).start()

            return carry

        lax.fori_loop(0, 2, correct, 0)
        return carry

    lax.fori_loop(0, layers, layer_step, 0)
    lax.fori_loop(windows[2], blocks, bulk_block, 0)

    def whole(src, dst, sends, receives):
        return pltpu.make_async_remote_copy(
            src_ref=src.at[pl.ds(0, parts - 1)],
            dst_ref=dst.at[pl.ds(0, parts - 1)],
            send_sem=sends,
            recv_sem=receives,
            device_id=(px, py),
            device_id_type=MESH,
        )

    whole(slots, slot_in, slot_send, slot_recv).wait()
    landed = jnp.transpose(slot_in[:, 0, :])[:2, :]
    slots_out[...] = landed + (halves - 1) * 8 * (landed >> 3)

    def finish_bulk(block, carry):
        bulk_copy(block).wait()
        return carry

    lax.fori_loop(0, blocks, finish_bulk, 0)
    for side_index in range(4):
        correction_copy(side_index).wait()
        x, y, exists = neighbour(side_index)

        @pl.when(exists)
        def _():
            for layer in range(layers):
                trace_copy(layer, side_index, x, y).wait_send()

    whole(move_out, move_in, move_send, move_recv).wait()
    moved_out[pl.ds(0, parts)] = move_in[...]


def scatter_kernel(bulk, correction, moved, recv_list, slots, out, held, added, sems, added_sem, out_sems):
    chunks = sems.shape[0]
    tiles, halves = bulk.shape[:2]
    size = tiles // chunks
    held_flat = held.reshape(held.shape[0] * halves * 8, LANES)
    added_flat = added.reshape(added.shape[0] * halves * 8, LANES)

    def bulk_copy(chunk):
        part = pl.ds(chunk * size, size)
        return pltpu.make_async_copy(bulk.at[part], held.at[part], sems.at[chunk])

    def out_copy(chunk, half):
        part = pl.ds(chunk * size, size)
        return pltpu.make_async_copy(
            held.at[part, half], out.at[part, :, pl.ds(half * LANES, LANES)], out_sems.at[chunk, half]
        )

    added_copy = pltpu.make_async_copy(correction, added.at[pl.ds(0, correction.shape[0])], added_sem)
    added_copy.start()
    for chunk in range(chunks):
        bulk_copy(chunk).start()
    added_copy.wait()
    for chunk in range(chunks):
        bulk_copy(chunk).wait()

    def add(line, carry):
        for batch in range(LANES // BATCH):
            first = pl.multiple_of((line * LANES + batch * BATCH) * halves, BATCH * halves)
            source = added_flat.at[pl.ds(first, BATCH * halves + SPARE * 8)]
            start = batch * BATCH
            last = recv_list[line, start + BATCH - 1]

            @pl.when(last < MARK)
            def _():
                spots = [recv_list[line, start + inner] for inner in range(BATCH)]
                sums = []
                for inner, spot in enumerate(spots):
                    own = source[pl.ds(inner // 8 * 8 * halves + inner % 8, halves, stride=8), :]
                    sums.append(held_flat[pl.ds(spot, halves, stride=8), :] + own)
                for spot, value in zip(spots, sums):
                    held_flat[pl.ds(spot, halves, stride=8), :] = value

            @pl.when(last >= MARK)
            def _():
                def one(inner, carry):
                    spot = recv_list[line, start + inner] & (MARK - 1)
                    own = added_flat[pl.ds(first + inner // 8 * 8 * halves + lax.rem(inner, 8), halves, stride=8), :]
                    held_flat[pl.ds(spot, halves, stride=8), :] = held_flat[pl.ds(spot, halves, stride=8), :] + own
                    return carry

                lax.fori_loop(0, BATCH, one, 0)

        return carry

    lax.fori_loop(0, recv_list.shape[0], add, 0)

    for which in range(2):
        for source in range(slots.shape[1]):
            spot = slots[which, source]
            held_flat[pl.ds(spot, halves, stride=8), :] = moved[source, pl.ds(halves * which, halves), :]
    for chunk in range(chunks):
        for half in range(halves):
            out_copy(chunk, half).start()
    for chunk in range(chunks):
        for half in range(halves):
            out_copy(chunk, half).wait()


VMEM = pl.BlockSpec(memory_space=pltpu.VMEM)
SMEM = pl.BlockSpec(memory_space=pltpu.SMEM)
ANY = pl.BlockSpec(memory_space=pl.ANY)
LIMIT = 60 * 1024 * 1024


def local(
    state,
    prop_base,
    prop_height,
    restrict,
    lift,
    layer_id,
    heights,
    degree,
    send_rows,
    recv_rows,
    move_src,
    move_dst,
    move_slot,
):
    parts_x, parts_y = lax.axis_size("px"), lax.axis_size("py")
    parts = parts_x * parts_y
    current = state[0, 0]
    count, width = current.shape
    halves = width // LANES
    layers = 3
    to_send, to_take = send_rows[0, 0], recv_rows[0, 0]
    sent = to_take.size
    total = sent + 2 * parts
    blocks = count // ROWS
    windows = (blocks * 2 // 8, blocks * 4 // 8, blocks * 6 // 8)
    bulk, correction, moved, slots, marked = pl.pallas_call(
        functools.partial(layers_kernel, parts_x, parts_y, layers, windows),
        name="layers",
        out_shape=(
            jax.ShapeDtypeStruct((count // 8, halves, 8, LANES), F32),
            jax.ShapeDtypeStruct((sent // 8, halves, 8, LANES), F32),
            jax.ShapeDtypeStruct((parts + SPARE, 4, LANES), F32),
            jax.ShapeDtypeStruct((2, parts), jnp.int32),
            jax.ShapeDtypeStruct((sent // LANES, LANES), jnp.int32),
        ),
        in_specs=[ANY] + [VMEM] * 12,
        out_specs=(ANY, ANY, VMEM, VMEM, VMEM),
        scratch_shapes=[
            pltpu.VMEM((total // 8 + SPARE, halves + 1, 8, LANES), F32),
            pltpu.VMEM((count // 8 + SPARE, halves + 1, 8, LANES), F32),
            pltpu.VMEM((sent + 8, LANES), F32),
            pltpu.VMEM((sent // 8, halves, 8, LANES), F32),
            pltpu.VMEM((total, sent), BF16),
            pltpu.VMEM((layers, total, LANES), F32),
            pltpu.VMEM((layers, sent, LANES), F32),
            pltpu.VMEM((sent, 2 * LANES), BF16),
            pltpu.VMEM((3 * width, 2 * width), BF16),
            pltpu.VMEM((width, 2 * LANES), BF16),
            pltpu.VMEM((3 * LANES, width), BF16),
            pltpu.VMEM((3 * LANES, 2 * width), BF16),
            pltpu.VMEM((PLACE_RECV + sent // LANES, LANES), jnp.int32),
            pltpu.SMEM((PLACE_RECV + sent // LANES, LANES), jnp.int32),
            pltpu.VMEM((total // LANES, LANES), jnp.int32),
            pltpu.VMEM((sent // LANES, LANES), jnp.int32),
            pltpu.VMEM((parts, 1, LANES), jnp.int32),
            pltpu.VMEM((parts, 4, LANES), F32),
            pltpu.VMEM((parts, 4, LANES), F32),
            pltpu.VMEM((parts, 1, LANES), jnp.int32),
            pltpu.SemaphoreType.DMA((layers, 4)),
            pltpu.SemaphoreType.DMA((layers, 4)),
            pltpu.SemaphoreType.DMA((4, halves)),
            pltpu.SemaphoreType.DMA,
            pltpu.SemaphoreType.DMA((blocks,)),
            pltpu.SemaphoreType.DMA((4,)),
            pltpu.SemaphoreType.DMA,
            pltpu.SemaphoreType.DMA,
            pltpu.SemaphoreType.DMA,
            pltpu.SemaphoreType.DMA,
        ],
        compiler_params=pltpu.CompilerParams(vmem_limit_bytes=LIMIT, collective_id=0, has_side_effects=True),
    )(
        current.reshape(count // 8, 8, width),
        layer_id[0],
        heights[0],
        degree[0],
        to_send,
        to_take,
        move_dst[0],
        move_src[0],
        move_slot[0],
        prop_base,
        prop_height,
        restrict,
        lift,
    )
    result = pl.pallas_call(
        scatter_kernel,
        name="scatter_rows",
        out_shape=jax.ShapeDtypeStruct((count // 8, 8, width), F32),
        in_specs=[ANY, ANY, VMEM, SMEM, SMEM],
        out_specs=ANY,
        scratch_shapes=[
            pltpu.VMEM((count // 8 + 1 + SPARE, halves, 8, LANES), F32),
            pltpu.VMEM((sent // 8 + SPARE, halves, 8, LANES), F32),
            pltpu.SemaphoreType.DMA((4,)),
            pltpu.SemaphoreType.DMA,
            pltpu.SemaphoreType.DMA((4, halves)),
        ],
        compiler_params=pltpu.CompilerParams(vmem_limit_bytes=LIMIT),
    )(bulk, correction, moved, marked, slots)
    return result.reshape(count, width)[None, None]


def solution(mesh):
    in_specs = (
        P("px", "py", None, None),
        P(),
        P(),
        P(),
        P(),
        P("px", "py", None),
        P("px", "py", None),
        P("px", "py", None),
        P("px", "py", None, None),
        P("px", "py", None, None),
        P("px", "py", None),
        P("px", "py", None),
        P("px", "py", None),
    )
    out_specs = P("px", "py", None, None)
    return jax.shard_map(local, mesh=mesh, in_specs=in_specs, out_specs=out_specs, check_vma=False)
```

```python
import functools

import jax
import jax.numpy as jnp
from jax import lax
from jax.experimental import pallas as pl
from jax.experimental.pallas import tpu as pltpu
from jax.sharding import PartitionSpec as P

MESH = pl.DeviceIdType.MESH
F32 = jnp.float32
BF16 = jnp.bfloat16
LANES = 128
ROWS = 1024
MARK = 1 << 20
BATCH = 16
PLACE_RECV = 24
SPARE = 8


def split(value):
    high = value.astype(BF16)
    return high, (value - high.astype(F32)).astype(BF16)


def pieces(values):
    pairs = [split(value) for value in values]
    high = [pair[0] for pair in pairs]
    return jnp.concatenate(high + [pair[1] for pair in pairs] + high, axis=1)


def weights(value):
    high, low = split(value)
    return jnp.concatenate([high, high, low], axis=0)


def product(left, right):
    return jnp.dot(left, right, preferred_element_type=F32)


def column(row):
    return jnp.transpose(jnp.broadcast_to(row, (LANES, LANES)))


def layers_kernel(
    parts_x,
    parts_y,
    layers,
    windows,
    state,
    layer_id,
    heights,
    degree,
    send_rows,
    recv_rows,
    target,
    leaving,
    landing,
    base,
    height,
    restrict,
    lift,
    bulk_out,
    correction_out,
    moved_out,
    slots_out,
    recv_out,
    rows,
    held,
    recv_meta,
    correction,
    match,
    trace,
    arrived,
    arrived_pieces,
    prop_w,
    restrict_w,
    lift_w,
    through_w,
    places,
    place_list,
    flat_ids,
    flat_recv,
    slots,
    move_out,
    move_in,
    slot_in,
    send_sem,
    recv_sem,
    state_sem,
    list_sem,
    bulk_sem,
    correction_sem,
    slot_send,
    slot_recv,
    move_send,
    move_recv,
):
    px, py = lax.axis_index("px"), lax.axis_index("py")
    parts = parts_x * parts_y
    me = px * parts_y + py
    count, width = state.shape[0] * 8, state.shape[2]
    sent = arrived.shape[1]
    side = sent // 4
    moves = 2 * parts
    halves = width // LANES
    groups = halves + 1
    held_flat = held.reshape(held.shape[0] * 8 * groups, LANES)
    rows_flat = rows.reshape(rows.shape[0] * 8 * groups, LANES)
    blocks = count // ROWS
    chunks = state_sem.shape[0]

    barrier = pltpu.get_barrier_semaphore()

    def each_other(action):
        def at_x(dx, carry):
            x = px + dx
            x = jnp.where(x >= parts_x, x - parts_x, x)
            for dy in range(parts_y):
                y = py + dy
                action(x, jnp.where(y >= parts_y, y - parts_y, y))
            return carry

        lax.fori_loop(1, parts_x, at_x, 0)
        for dy in range(1, parts_y):
            y = py + dy
            action(px, jnp.where(y >= parts_y, y - parts_y, y))

    def greet(x, y):
        pl.semaphore_signal(barrier, inc=1, device_id=(x, y), device_id_type=MESH)

    def state_copy(chunk, half):
        part = pl.ds(chunk * (count // 8 // chunks), count // 8 // chunks)
        return pltpu.make_async_copy(
            state.at[part, :, pl.ds(half * LANES, LANES)], held.at[part, half], state_sem.at[chunk, half]
        )

    for chunk in range(chunks):
        for half in range(halves):
            state_copy(chunk, half).start()
    each_other(greet)

    def neighbour(side_index):
        dx = jnp.where(side_index == 0, 1, jnp.where(side_index == 1, -1, 0))
        dy = jnp.where(side_index == 2, 1, jnp.where(side_index == 3, -1, 0))
        x, y = px + dx, py + dy
        exists = (x >= 0) & (x < parts_x) & (y >= 0) & (y < parts_y)
        return x, y, exists

    def source_exists(side_index):
        dx = jnp.where(side_index == 0, -1, jnp.where(side_index == 1, 1, 0))
        dy = jnp.where(side_index == 2, -1, jnp.where(side_index == 3, 1, 0))
        x, y = px + dx, py + dy
        return (x >= 0) & (x < parts_x) & (y >= 0) & (y < parts_y)

    def trace_copy(layer, side_index, x, y):
        part = pl.ds(pl.multiple_of(side_index * side, side), side)
        return pltpu.make_async_remote_copy(
            src_ref=trace.at[layer, part],
            dst_ref=arrived.at[layer, part],
            send_sem=send_sem.at[layer, side_index],
            recv_sem=recv_sem.at[layer, side_index],
            device_id=(x, y),
            device_id_type=MESH,
        )

    def send_side(layer, side_index):
        x, y, exists = neighbour(side_index)

        @pl.when(exists)
        def _():
            trace_copy(layer, side_index, x, y).start()

    lane = lax.broadcasted_iota(jnp.int32, (LANES, LANES), 1)
    item = lax.broadcasted_iota(jnp.int32, (LANES, LANES), 0)
    to = column(target[...])
    earlier = (to == target[...]) & (item < lane)
    place = column(jnp.sum(jnp.where(earlier, 1, 0), axis=0, keepdims=True))
    source_of = column(leaving[...])
    landing_of = column(landing[...]) - count
    spread_slots = []
    for which in range(2):
        chosen = (to == lane) & (place == which)
        ids = jnp.sum(jnp.where(chosen, source_of, 0), axis=0, keepdims=True)
        flat_ids[pl.ds(sent // LANES + which, 1), :] = ids
        slot = count + jnp.sum(jnp.where(chosen, landing_of, 0), axis=0, keepdims=True)
        spread_slots.append(column(slot))
        flat_ids[pl.ds(sent // LANES + which, 1), :] = ids.astype(jnp.int32)
    for index in range(sent // LANES):
        side_index, start = index * LANES // side, index * LANES % side
        flat_ids[pl.ds(index, 1), :] = send_rows[side_index : side_index + 1, start : start + LANES]
        flat_recv[pl.ds(index, 1), :] = recv_rows[side_index : side_index + 1, start : start + LANES]
    places[pl.ds(0, flat_ids.shape[0]), :] = flat_ids[...] + (groups - 1) * 8 * (flat_ids[...] >> 3)
    received = flat_recv[...]
    places[pl.ds(PLACE_RECV, received.shape[0]), :] = received + (groups - 1) * 8 * (received >> 3)
    list_copy = pltpu.make_async_copy(places, place_list, list_sem)
    list_copy.start()
    slots[:, 0, :] = jnp.where(lane == 0, spread_slots[0], spread_slots[1])

    place_in_batch = lax.broadcasted_iota(jnp.int32, received.shape, 1) & (BATCH - 1)
    marks = jnp.zeros(received.shape, F32)
    for shift in range(1, BATCH):
        same = (received == pltpu.roll(received, shift, 1)) & (place_in_batch >= shift)
        marks = jnp.where(same, 1.0, marks)
    shift = 1
    while shift < BATCH:
        marks = jnp.maximum(marks, pltpu.roll(marks, shift, 1))
        shift *= 2
    spots = received + (halves - 1) * 8 * (received >> 3)
    recv_out[...] = spots + jnp.where((place_in_batch == BATCH - 1) & (marks > 0.5), MARK, 0)

    restrict_high, restrict_low = split(restrict[...])
    restrict_w[:, pl.ds(0, LANES)] = restrict_high
    restrict_w[:, pl.ds(LANES, LANES)] = restrict_low

    def spread(block, carry):
        part = pl.ds(pl.multiple_of(block * (LANES // 8), LANES // 8), LANES // 8)
        cols = pl.ds(pl.multiple_of(block * LANES, LANES), LANES)
        info = layer_id[:, cols] + 4 * heights[:, cols] + 32 * degree[:, cols]
        held[part, halves] = column(info.astype(F32)).reshape(LANES // 8, 8, LANES)
        return carry

    lax.fori_loop(0, count // LANES, spread, 0, unroll=4)

    def traced(values):
        pairs = [split(value) for value in values]
        high = jnp.concatenate([pair[0] for pair in pairs], axis=1)
        low = jnp.concatenate([pair[1] for pair in pairs], axis=1)
        both = product(high, restrict_w[...])
        return both[:, :LANES] + both[:, LANES:] + product(low, restrict_w[:, pl.ds(0, LANES)])

    def read(ref, first, size, which):
        part = pl.ds(pl.multiple_of(first // 8, LANES // 8), size // 8)
        return ref[part, which].reshape(size, LANES)

    def write(ref, first, size, values):
        part = pl.ds(pl.multiple_of(first // 8, LANES // 8), size // 8)
        for which, value in enumerate(values):
            ref[part, which] = value.reshape(size // 8, 8, LANES)

    def read_row(ref, first, size):
        return [read(ref, first, size, half) for half in range(halves)]

    list_copy.wait()
    for chunk in range(chunks):
        for half in range(halves):
            state_copy(chunk, half).wait()

    def take(line, carry):
        into = rows_flat.at[pl.ds(pl.multiple_of(line * (LANES * groups), LANES * groups), LANES * groups + SPARE * 8)]
        for inner in range(LANES):
            spot = inner // 8 * 8 * groups + inner % 8
            into[pl.ds(spot, groups, stride=8), :] = held_flat[pl.ds(place_list[line, inner], groups, stride=8), :]
        return carry

    for side_index in range(4):
        lax.fori_loop(side_index * (side // LANES), (side_index + 1) * (side // LANES), take, 0)
        trace[0, pl.ds(side_index * side, side), :] = traced(read_row(rows, side_index * side, side))

    prop_w[:, pl.ds(0, width)] = weights(base[...])
    prop_w[:, pl.ds(width, width)] = weights(height[...])
    lift_w[...] = weights(lift[...])
    through = product(pieces([lift[:, half * LANES : (half + 1) * LANES] for half in range(halves)]), prop_w[...])
    through_w[...] = weights(through)

    pl.semaphore_wait(barrier, parts - 1)
    for side_index in range(4):
        send_side(0, side_index)

    def slot_copy(x, y):
        return pltpu.make_async_remote_copy(
            src_ref=slots.at[x * parts_y + y],
            dst_ref=slot_in.at[me],
            send_sem=slot_send,
            recv_sem=slot_recv,
            device_id=(x, y),
            device_id_type=MESH,
        )

    def move_copy(x, y):
        return pltpu.make_async_remote_copy(
            src_ref=move_out.at[x * parts_y + y],
            dst_ref=move_in.at[me],
            send_sem=move_send,
            recv_sem=move_recv,
            device_id=(x, y),
            device_id_type=MESH,
        )

    each_other(lambda x, y: slot_copy(x, y).start())
    slot_in[pl.ds(me, 1)] = jnp.full((1, 1, LANES), count, jnp.int32)
    move_in[pl.ds(me, 1)] = jnp.zeros((1, 4, LANES), F32)

    lax.fori_loop(sent // LANES, (sent + moves) // LANES, take, 0)

    def take_meta(line, carry):
        into = recv_meta.at[pl.ds(pl.multiple_of(line * LANES, LANES), LANES)]
        for inner in range(LANES):
            place = place_list[line + PLACE_RECV, inner]
            into[inner : inner + 1, :] = held_flat[pl.ds(place + 8 * halves, 1), :]
        return carry

    lax.fori_loop(0, sent // LANES, take_meta, 0)
    for side_index in range(4):

        @pl.when(jnp.logical_not(source_exists(side_index)))
        def _():
            for layer in range(layers):
                arrived[layer, pl.ds(side_index * side, side), :] = jnp.zeros((side, LANES), F32)

    def match_rows_of(row, part):
        ids = column(row)
        for group in range(sent // LANES):
            same = ids == flat_recv[group : group + 1, :]
            match[part, pl.ds(group * LANES, LANES)] = jnp.where(same, 1.0, 0.0).astype(BF16)

    def build_match(block, carry):
        match_rows_of(flat_ids[pl.ds(block, 1), :], pl.ds(pl.multiple_of(block * LANES, LANES), LANES))
        return carry

    lax.fori_loop(0, (sent + moves) // LANES, build_match, 0)

    def finish(both, old, packed, layer):
        info = packed.astype(jnp.int32)
        scale = ((info >> 2) & 7).astype(F32) * 0.25
        active = (info >> 5) * (width // 4)
        pitched = (info & 3) <= layer
        lane = lax.broadcasted_iota(jnp.int32, info.shape, 1)
        values = []
        for half in range(halves):
            start = half * LANES
            value = both[:, start : start + LANES] + scale * both[:, width + start : width + start + LANES]
            value = jnp.where(lane + start < active, value, 0.0)
            values.append(jnp.where(pitched, value, 0.0 if old is None else old[half]))
        return values

    def advance(old, combined, packed, layer):
        return finish(product(pieces(combined), prop_w[...]), old, packed, layer)

    def bulk_copy(block):
        part = pl.ds(pl.multiple_of(block * (ROWS // 8), ROWS // 8), ROWS // 8)
        return pltpu.make_async_copy(held.at[part, pl.ds(0, halves)], bulk_out.at[part], bulk_sem.at[block])

    def bulk_block(block, carry):
        first = block * ROWS

        def one(layer, carry):
            values = read_row(held, first, ROWS)
            write(held, first, ROWS, advance(values, values, read(held, first, ROWS, halves), layer))
            return carry

        lax.fori_loop(0, layers, one, 0)
        bulk_copy(block).start()
        return carry

    def plus(values, added):
        return [value + added[:, half * LANES : (half + 1) * LANES] for half, value in enumerate(values)]

    def compact(first, size, layer):
        parts_of = -(-size // 512)
        step = size // parts_of
        inflows = []
        for index in range(parts_of):
            part = pl.ds(pl.multiple_of(first + index * step, LANES), step)
            inflow = product(match[part, :], arrived_pieces[...])
            inflows.append(inflow[:, :LANES] + inflow[:, LANES:])
        lifted = jnp.concatenate([product(pieces([inflow]), lift_w[...]) for inflow in inflows], axis=0)
        old = read_row(rows, first, size)
        new = advance(old, plus(old, lifted), read(rows, first, size, halves), layer)
        write(rows, first, size, new)
        return new

    def correction_copy(side_index):
        part = pl.ds(pl.multiple_of(side_index * (side // 8), side // 8), side // 8)
        return pltpu.make_async_copy(correction.at[part], correction_out.at[part], correction_sem.at[side_index])

    def layer_step(layer, carry):
        first = jnp.where(layer == 0, 0, jnp.where(layer == 1, windows[0], windows[1]))
        last = jnp.where(layer == 0, windows[0], jnp.where(layer == 1, windows[1], windows[2]))
        lax.fori_loop(first, last, bulk_block, 0)
        for side_index in range(4):

            @pl.when(source_exists(side_index))
            def _():
                trace_copy(layer, side_index, px, py).wait_recv()

        def cut(side_index, carry):
            part = pl.ds(pl.multiple_of(side_index * side, side), side)
            high, low = split(arrived[layer, part, :])
            arrived_pieces[part, pl.ds(0, LANES)] = high
            arrived_pieces[part, pl.ds(LANES, LANES)] = low
            return carry

        lax.fori_loop(0, 4, cut, 0)

        @pl.when(layer < layers - 1)
        def _():
            size = (sent + moves) // 2

            def two_sides(pair, carry):
                trace[layer + 1, pl.ds(pl.multiple_of(pair * size, LANES), size), :] = traced(
                    compact(pair * size, size, layer)
                )
                send_side(layer + 1, 2 * pair)
                send_side(layer + 1, 2 * pair + 1)
                return carry

            lax.fori_loop(0, 2, two_sides, 0)

        @pl.when(layer == layers - 1)
        def _():
            leaving_rows = compact(sent, moves, layer)
            for which in range(2):
                for half in range(halves):
                    move_out[:, halves * which + half, :] = leaving_rows[half][which * parts : (which + 1) * parts]
            each_other(lambda x, y: move_copy(x, y).start())

        def correct(pair, carry):
            part = pl.ds(pl.multiple_of(pair * 2 * side, 2 * side), 2 * side)
            high = arrived_pieces[part, pl.ds(0, LANES)]
            low = arrived_pieces[part, pl.ds(LANES, LANES)]
            triple = jnp.concatenate([high, low, high], axis=1)
            info = recv_meta[part, :]
            first = pair * 2 * side

            @pl.when(layer == 0)
            def _():
                write(correction, first, 2 * side, finish(product(triple, through_w[...]), None, info, layer))

            @pl.when(layer > 0)
            def _():
                old = read_row(correction, first, 2 * side)
                new = advance(old, plus(old, product(triple, lift_w[...])), info, layer)
                write(correction, first, 2 * side, new)

            @pl.when(layer == layers - 1)
            def _():
                correction_copy(2 * pair).start()
                correction_copy(2 * pair + 1).start()

            return carry

        lax.fori_loop(0, 2, correct, 0)
        return carry

    lax.fori_loop(0, layers, layer_step, 0)
    lax.fori_loop(windows[2], blocks, bulk_block, 0)

    def whole(src, dst, sends, receives):
        return pltpu.make_async_remote_copy(
            src_ref=src.at[pl.ds(0, parts - 1)],
            dst_ref=dst.at[pl.ds(0, parts - 1)],
            send_sem=sends,
            recv_sem=receives,
            device_id=(px, py),
            device_id_type=MESH,
        )

    whole(slots, slot_in, slot_send, slot_recv).wait()
    landed = jnp.transpose(slot_in[:, 0, :])[:2, :]
    slots_out[...] = landed + (halves - 1) * 8 * (landed >> 3)

    def finish_bulk(block, carry):
        bulk_copy(block).wait()
        return carry

    lax.fori_loop(0, blocks, finish_bulk, 0)
    for side_index in range(4):
        correction_copy(side_index).wait()
        x, y, exists = neighbour(side_index)

        @pl.when(exists)
        def _():
            for layer in range(layers):
                trace_copy(layer, side_index, x, y).wait_send()

    whole(move_out, move_in, move_send, move_recv).wait()
    moved_out[pl.ds(0, parts)] = move_in[...]


def scatter_kernel(bulk, correction, moved, recv_list, slots, out, held, added, sems, added_sem, out_sems):
    chunks = sems.shape[0]
    tiles, halves = bulk.shape[:2]
    size = tiles // chunks
    held_flat = held.reshape(held.shape[0] * halves * 8, LANES)
    added_flat = added.reshape(added.shape[0] * halves * 8, LANES)

    def bulk_copy(chunk):
        part = pl.ds(chunk * size, size)
        return pltpu.make_async_copy(bulk.at[part], held.at[part], sems.at[chunk])

    def out_copy(chunk, half):
        part = pl.ds(chunk * size, size)
        return pltpu.make_async_copy(
            held.at[part, half], out.at[part, :, pl.ds(half * LANES, LANES)], out_sems.at[chunk, half]
        )

    added_copy = pltpu.make_async_copy(correction, added.at[pl.ds(0, correction.shape[0])], added_sem)
    added_copy.start()
    for chunk in range(chunks):
        bulk_copy(chunk).start()
    added_copy.wait()
    for chunk in range(chunks):
        bulk_copy(chunk).wait()

    def add(line, carry):
        for batch in range(LANES // BATCH):
            first = pl.multiple_of((line * LANES + batch * BATCH) * halves, BATCH * halves)
            source = added_flat.at[pl.ds(first, BATCH * halves + SPARE * 8)]
            start = batch * BATCH
            last = recv_list[line, start + BATCH - 1]

            @pl.when(last < MARK)
            def _():
                spots = [recv_list[line, start + inner] for inner in range(BATCH)]
                sums = []
                for inner, spot in enumerate(spots):
                    own = source[pl.ds(inner // 8 * 8 * halves + inner % 8, halves, stride=8), :]
                    sums.append(held_flat[pl.ds(spot, halves, stride=8), :] + own)
                for spot, value in zip(spots, sums):
                    held_flat[pl.ds(spot, halves, stride=8), :] = value

            @pl.when(last >= MARK)
            def _():
                def one(inner, carry):
                    spot = recv_list[line, start + inner] & (MARK - 1)
                    own = added_flat[pl.ds(first + inner // 8 * 8 * halves + lax.rem(inner, 8), halves, stride=8), :]
                    held_flat[pl.ds(spot, halves, stride=8), :] = held_flat[pl.ds(spot, halves, stride=8), :] + own
                    return carry

                lax.fori_loop(0, BATCH, one, 0)

        return carry

    lax.fori_loop(0, recv_list.shape[0], add, 0)

    for which in range(2):
        for source in range(slots.shape[1]):
            spot = slots[which, source]
            held_flat[pl.ds(spot, halves, stride=8), :] = moved[source, pl.ds(halves * which, halves), :]
    for chunk in range(chunks):
        for half in range(halves):
            out_copy(chunk, half).start()
    for chunk in range(chunks):
        for half in range(halves):
            out_copy(chunk, half).wait()


VMEM = pl.BlockSpec(memory_space=pltpu.VMEM)
SMEM = pl.BlockSpec(memory_space=pltpu.SMEM)
ANY = pl.BlockSpec(memory_space=pl.ANY)
LIMIT = 60 * 1024 * 1024


def local(
    state,
    prop_base,
    prop_height,
    restrict,
    lift,
    layer_id,
    heights,
    degree,
    send_rows,
    recv_rows,
    move_src,
    move_dst,
    move_slot,
):
    parts_x, parts_y = lax.axis_size("px"), lax.axis_size("py")
    parts = parts_x * parts_y
    current = state[0, 0]
    count, width = current.shape
    halves = width // LANES
    layers = 3
    to_send, to_take = send_rows[0, 0], recv_rows[0, 0]
    sent = to_take.size
    total = sent + 2 * parts
    blocks = count // ROWS
    windows = (blocks // 8, blocks * 3 // 8, blocks * 5 // 8)
    bulk, correction, moved, slots, marked = pl.pallas_call(
        functools.partial(layers_kernel, parts_x, parts_y, layers, windows),
        name="layers",
        out_shape=(
            jax.ShapeDtypeStruct((count // 8, halves, 8, LANES), F32),
            jax.ShapeDtypeStruct((sent // 8, halves, 8, LANES), F32),
            jax.ShapeDtypeStruct((parts + SPARE, 4, LANES), F32),
            jax.ShapeDtypeStruct((2, parts), jnp.int32),
            jax.ShapeDtypeStruct((sent // LANES, LANES), jnp.int32),
        ),
        in_specs=[ANY] + [VMEM] * 12,
        out_specs=(ANY, ANY, VMEM, VMEM, VMEM),
        scratch_shapes=[
            pltpu.VMEM((total // 8 + SPARE, halves + 1, 8, LANES), F32),
            pltpu.VMEM((count // 8 + SPARE, halves + 1, 8, LANES), F32),
            pltpu.VMEM((sent + 8, LANES), F32),
            pltpu.VMEM((sent // 8, halves, 8, LANES), F32),
            pltpu.VMEM((total, sent), BF16),
            pltpu.VMEM((layers, total, LANES), F32),
            pltpu.VMEM((layers, sent, LANES), F32),
            pltpu.VMEM((sent, 2 * LANES), BF16),
            pltpu.VMEM((3 * width, 2 * width), BF16),
            pltpu.VMEM((width, 2 * LANES), BF16),
            pltpu.VMEM((3 * LANES, width), BF16),
            pltpu.VMEM((3 * LANES, 2 * width), BF16),
            pltpu.VMEM((PLACE_RECV + sent // LANES, LANES), jnp.int32),
            pltpu.SMEM((PLACE_RECV + sent // LANES, LANES), jnp.int32),
            pltpu.VMEM((total // LANES, LANES), jnp.int32),
            pltpu.VMEM((sent // LANES, LANES), jnp.int32),
            pltpu.VMEM((parts, 1, LANES), jnp.int32),
            pltpu.VMEM((parts, 4, LANES), F32),
            pltpu.VMEM((parts, 4, LANES), F32),
            pltpu.VMEM((parts, 1, LANES), jnp.int32),
            pltpu.SemaphoreType.DMA((layers, 4)),
            pltpu.SemaphoreType.DMA((layers, 4)),
            pltpu.SemaphoreType.DMA((4, halves)),
            pltpu.SemaphoreType.DMA,
            pltpu.SemaphoreType.DMA((blocks,)),
            pltpu.SemaphoreType.DMA((4,)),
            pltpu.SemaphoreType.DMA,
            pltpu.SemaphoreType.DMA,
            pltpu.SemaphoreType.DMA,
            pltpu.SemaphoreType.DMA,
        ],
        compiler_params=pltpu.CompilerParams(vmem_limit_bytes=LIMIT, collective_id=0, has_side_effects=True),
    )(
        current.reshape(count // 8, 8, width),
        layer_id[0],
        heights[0],
        degree[0],
        to_send,
        to_take,
        move_dst[0],
        move_src[0],
        move_slot[0],
        prop_base,
        prop_height,
        restrict,
        lift,
    )
    result = pl.pallas_call(
        scatter_kernel,
        name="scatter_rows",
        out_shape=jax.ShapeDtypeStruct((count // 8, 8, width), F32),
        in_specs=[ANY, ANY, VMEM, SMEM, SMEM],
        out_specs=ANY,
        scratch_shapes=[
            pltpu.VMEM((count // 8 + 1 + SPARE, halves, 8, LANES), F32),
            pltpu.VMEM((sent // 8 + SPARE, halves, 8, LANES), F32),
            pltpu.SemaphoreType.DMA((4,)),
            pltpu.SemaphoreType.DMA,
            pltpu.SemaphoreType.DMA((4, halves)),
        ],
        compiler_params=pltpu.CompilerParams(vmem_limit_bytes=LIMIT),
    )(bulk, correction, moved, marked, slots)
    return result.reshape(count, width)[None, None]


def solution(mesh):
    in_specs = (
        P("px", "py", None, None),
        P(),
        P(),
        P(),
        P(),
        P("px", "py", None),
        P("px", "py", None),
        P("px", "py", None),
        P("px", "py", None, None),
        P("px", "py", None, None),
        P("px", "py", None),
        P("px", "py", None),
        P("px", "py", None),
    )
    out_specs = P("px", "py", None, None)
    return jax.shard_map(local, mesh=mesh, in_specs=in_specs, out_specs=out_specs, check_vma=False)
```
